512 devices in a mesh: band: 16 (over y, core), ma: 32 (over z, x).
Axes of the slice: x: 4, y: 8, z: 8, core: 2. Of those that a mesh axis runs over, the one named last changes fastest.
Arguments:
- coeffs: bfloat16 [64, 2048, 48], P('ma'), may hold values from -6 to 6
- tables: bfloat16 [64, 2, 256, 2048], P('ma'), may hold values from -0.005859375 to 0.005859375
- beam: float32 [16, 2048], P('band'), may hold values from 0.2 to 1
- mixing: float32 [16, 3, 256, 4096], P('band', None, 'ma'), may hold values from 0.3 to 1.5
- noise_diag: float32 [16, 2, 256, 4096], P('band', None, 'ma'), may hold values from 0.05 to 0.2
- noise_cross: float32 [16, 256, 4096], P('band', 'ma'), may hold values from -0.04 to 0.04
- prior: float32 [6, 2048], P(None, 'band'), may hold values from 0.3 to 3
- m_values: int32 [64], replicated, may hold values from 0 to 63, as said below
- cycle_ids: int32 [256], P('ma'), may hold values from 0 to 255, each once
Outputs:
- product: float32 [64, 2048, 48], P('ma', 'band')
The draws below stay inside these ranges and needn't reach their ends.
Inputs may be any that keep to these rules, and one draw needn't show every extreme that they name: `m_values`: each of 0 to 63 appears once; slots 2k and 2k + 1 hold m and 63 - m. `cycle_ids`: each cycle number appears once.
All inputs are finite; a program needn't handle non-finite values.
Results may differ from the reference program's by a relative error of at most 0.0015.
Values may be sent and summed in bfloat16 or wider, within the bound.
No kernel may reach another device: no remote copies, remote signals or barrier semaphores. Data moves between devices by JAX's collectives and lax.ppermute only.
A program may use at most 64 MiB of HBM per device.

```python
import math
import jax
import jax.numpy as jnp
from jax import lax

L = 2048
PIX = 4096
COMPS = 3
CHAINS = 4
MODES = 64
CYCLES = 256
BANDS = 16
COLS = 48


def draw_m_values(key, part):
    low_half = jax.random.permutation(key, MODES // 2).astype(jnp.int32)
    return jnp.stack([low_half, MODES - 1 - low_half], axis=1).reshape(MODES).astype(jnp.int32)


def shard_levels(rng, shape, cuts, smallest, largest):
    def one(dim, parts):
        heights = jax.random.uniform(jax.random.fold_in(jax.random.fold_in(rng, 6), dim), (parts,), jnp.float32, smallest / len(cuts), largest / len(cuts))
        return jnp.repeat(jnp.exp(heights), shape[dim] // parts).reshape((-1,) + (1,) * (len(shape) - dim - 1))

    gain = one(*cuts[0])
    for cut in cuts[1:]:
        gain = gain * one(*cut)
    return gain


def bell_draw(rng, shape, deviation, reach, split=(), kind=jnp.bfloat16):
    drawn = deviation * jax.random.normal(rng, shape, jnp.float32)
    if split:
        drawn = drawn * shard_levels(rng, shape, split, -0.22, 0.18)
    return jnp.clip(drawn, -reach, reach).astype(kind)


def setup_inputs(seed: int = 0) -> dict:
    seeds = jax.random.split(jax.random.key(seed), 10)
    return {
        "coeffs": bell_draw(seeds[0], (MODES, L, COLS), 1.0, 6.0, ((0, 32),)),
        "tables": bell_draw(seeds[1], (MODES, 2, CYCLES, L), (CYCLES * PIX) ** -0.5, 0.005859375, ((0, 32),)),
        "beam": jnp.clip(jnp.exp(math.log(1.0) - 1.609438 * jax.random.uniform(seeds[2], (BANDS, L), jnp.float32) ** shard_levels(seeds[2], (BANDS, L), ((0, 16),), -0.2, 0.2)), 0.2, 1.0),
        "mixing": jnp.clip(jnp.exp(math.log(1.5) - 1.60943787 * jax.random.uniform(seeds[3], (BANDS, COMPS, CYCLES, PIX), jnp.float32) ** shard_levels(seeds[3], (BANDS, COMPS, CYCLES, PIX), ((0, 16), (2, 32)), -0.2, 0.2)), 0.3, 1.5),
        "noise_diag": jnp.clip(jnp.exp(math.log(0.2) - 1.3862944 * jax.random.uniform(seeds[4], (BANDS, 2, CYCLES, PIX), jnp.float32) ** shard_levels(seeds[4], (BANDS, 2, CYCLES, PIX), ((0, 16), (2, 32)), -0.2, 0.2)), 0.05, 0.2),
        "noise_cross": jnp.clip(jax.random.uniform(seeds[5], (BANDS, CYCLES, PIX), jnp.float32, -0.04, 0.04) * shard_levels(seeds[5], (BANDS, CYCLES, PIX), ((0, 16), (1, 32)), -0.4, 0.0), -0.04, 0.04),
        "prior": jnp.clip(jnp.exp(math.log(3.0) - 2.3025851 * jax.random.uniform(seeds[6], (2 * COMPS, L), jnp.float32) ** shard_levels(seeds[6], (2 * COMPS, L), ((1, 16),), -0.2, 0.2)), 0.3, 3.0),
        "m_values": draw_m_values(jax.random.fold_in(seeds[9], 71), 0),
        "cycle_ids": jax.random.permutation(seeds[8], CYCLES).astype(jnp.int32),
    }


def combine_pairs(plain_part, crossed):
    dims_all = plain_part.shape
    plain_part = plain_part.reshape(dims_all[:-1] + (dims_all[-1] // 4, 4))
    crossed = crossed.reshape(dims_all[:-1] + (dims_all[-1] // 4, 4))
    combined = jnp.stack([plain_part[..., 0] - crossed[..., 3], plain_part[..., 1] + crossed[..., 2],
                          plain_part[..., 2] + crossed[..., 1], plain_part[..., 3] - crossed[..., 0]], axis=-1)
    return combined.reshape(dims_all)


def trig_table(mode_ids, parity, pixels):
    offsets = 2 * jnp.arange(pixels, dtype=jnp.int32) + parity
    phase_index = (mode_ids[:, None] * offsets[None, :]) % (2 * pixels)
    angles = jnp.pi * phase_index.astype(jnp.float32) / pixels
    weight = jnp.where(mode_ids == 0, 1.0, 2.0).astype(jnp.float32)[:, None]
    return jnp.concatenate([weight * jnp.cos(angles), -weight * jnp.sin(angles)], 0).astype(jnp.bfloat16)


def reference(coeffs, tables, beam, mixing, noise_diag, noise_cross, prior, m_values, cycle_ids):
    fields = CHAINS * COMPS * 2
    running = jnp.zeros((MODES, L, COLS), jnp.float32)
    for band_index in range(BANDS):
        beamed = (coeffs.astype(jnp.float32) * beam[band_index][None, :, None]).astype(jnp.bfloat16)

        def synth(pair_in):
            table_pair, coef_block = pair_in
            stacked = jnp.dot(table_pair.reshape(2 * CYCLES, L), coef_block, preferred_element_type=jnp.float32)
            stacked = stacked.reshape(2, CYCLES, COLS)
            return combine_pairs(stacked[0], stacked[1]).astype(jnp.bfloat16)

        spectra = lax.map(synth, (tables, beamed))
        flattened = spectra.reshape(MODES, CYCLES, fields, 2).transpose(1, 2, 3, 0).reshape(CYCLES, fields, 2 * MODES)

        def cycle_work(item_in):
            flat_cycle, cycle_number, mix_cycle, diag_cycle, cross_cycle = item_in
            table = trig_table(m_values, cycle_number % 2, PIX)
            pixel_maps = jnp.dot(flat_cycle, table, preferred_element_type=jnp.float32).reshape(CHAINS, COMPS, 2, PIX)
            sky_map = jnp.sum(pixel_maps * mix_cycle[None, :, None, :], axis=1)
            weighted_q = diag_cycle[0] * sky_map[:, 0] + cross_cycle * sky_map[:, 1]
            weighted_u = cross_cycle * sky_map[:, 0] + diag_cycle[1] * sky_map[:, 1]
            weighted = jnp.stack([weighted_q, weighted_u], 1)
            returned_map = (weighted[:, None] * mix_cycle[None, :, None, :]).astype(jnp.bfloat16).reshape(fields, PIX)
            return jnp.dot(returned_map, table.T, preferred_element_type=jnp.float32).astype(jnp.bfloat16)

        returned = lax.map(cycle_work, (flattened, cycle_ids, mixing[band_index].transpose(1, 0, 2),
                                       noise_diag[band_index].transpose(1, 0, 2), noise_cross[band_index]))
        spectra_back = returned.reshape(CYCLES, fields, 2, MODES).transpose(3, 0, 1, 2).reshape(MODES, CYCLES, COLS)

        def adjoint(pair_in):
            table_pair, spec_block = pair_in
            plain_part = jnp.dot(table_pair[0].T, spec_block, preferred_element_type=jnp.float32)
            crossed = jnp.dot(table_pair[1].T, spec_block, preferred_element_type=jnp.float32)
            return combine_pairs(plain_part, crossed)

        partial_sum = lax.map(adjoint, (tables, spectra_back))
        running = running + partial_sum * beam[band_index][None, :, None]
    prior_cols = prior.reshape(COMPS, 2, L).transpose(2, 0, 1)
    prior_cols = jnp.broadcast_to(prior_cols[:, None, :, :, None], (L, CHAINS, COMPS, 2, 2)).reshape(L, COLS)
    return running + prior_cols[None] * coeffs.astype(jnp.float32)
```

```python
import math

import jax
import jax.numpy as jnp
from jax import lax
from jax.experimental import pallas as pl
from jax.experimental.pallas import tpu as pltpu
from jax.sharding import Mesh
from jax.sharding import PartitionSpec as P

F32 = jnp.float32
BF16 = jnp.bfloat16

PIX = 4096
COMPS = 3
CHAINS = 4
PAIRS = CHAINS * COMPS
COLS = 4 * PAIRS
SLOT = 16
PER = 8
PLACE = (0, 2, 1, 3)

NT = (((1,), (1,)), ((), ()))
NN = (((1,), (0,)), ((), ()))


def dot(a, b, dims):
    return lax.dot_general(a, b, dims, preferred_element_type=F32)


def crossed(slots):
    return [-slots[3], slots[2], slots[1], -slots[0]]


def synth_kernel(coef_ref, tab_ref, beam_ref, out_ref, nat_ref, acc_ref):
    step = pl.program_id(0)

    @pl.when(step == 0)
    def _():
        nat_ref[...] = jnp.zeros_like(nat_ref)

    total = None
    for s in range(2):
        beamed = (coef_ref[s].astype(F32) * beam_ref[...]).astype(BF16)
        tiles = range(beamed.shape[1] // 128)
        for j in tiles:
            nat_ref[s, j, :COLS, :] = beamed[:, j * 128 : (j + 1) * 128].astype(F32)
        slots = [
            jnp.concatenate([nat_ref[s, j, pl.ds(p, SLOT, stride=4), :] for j in tiles], 1)
            for p in PLACE
        ]
        none = jnp.zeros((4 * SLOT, beamed.shape[1]), BF16)
        for which, rows in enumerate((slots, crossed(slots))):
            rows = jnp.concatenate(rows, 0).astype(BF16)
            rows = jnp.concatenate([rows, none] if s == 0 else [none, rows], 0)
            part = dot(tab_ref[s, which], rows, NT)
            total = part if total is None else total + part

    @pl.when(step == 0)
    def _():
        acc_ref[...] = total

    @pl.when(step > 0)
    def _():
        acc_ref[...] += total

    @pl.when(step == pl.num_programs(0) - 1)
    def _():
        out_ref[...] = acc_ref[...].astype(BF16)


def synth(coeffs_t, tables, beam, chunks=4):
    _, cols, levels = coeffs_t.shape
    cycles = tables.shape[2]
    width = levels // chunks
    return pl.pallas_call(
        synth_kernel,
        out_shape=jax.ShapeDtypeStruct((cycles, 128), BF16),
        grid=(chunks,),
        in_specs=[
            pl.BlockSpec((2, cols, width), lambda k: (0, 0, k)),
            pl.BlockSpec((2, 2, cycles, width), lambda k: (0, 0, 0, k)),
            pl.BlockSpec((1, width), lambda k: (0, k)),
        ],
        out_specs=pl.BlockSpec((cycles, 128), lambda k: (0, 0)),
        scratch_shapes=[pltpu.VMEM((2, width // 128, 64, 128), F32), pltpu.VMEM((cycles, 128), F32)],
        name="synth",
    )(coeffs_t, tables, beam)


def iota(shape, dim):
    return lax.broadcasted_iota(jnp.int32, shape, dim)


def table_kernel(m_ref, out_ref):
    quarter = PIX // 4
    row = iota((32, 128), 0)
    mode, gain = [], []
    for s in range(2):
        m = jnp.zeros((32, 128), jnp.int32)
        for j in range(32):
            m = jnp.where(row == j, m_ref[2 * j + s], m)
        mode.append(m)
        gain.append(jnp.where(m == 0, 1.0, 2.0).astype(F32))
    lane = iota((32, 128), 1)

    def chunk(i, carry):
        first = i * 128
        for par in range(2):
            for s in range(2):
                k = (mode[s] * (2 * (lane + first) + par)) & (2 * PIX - 1)
                n = (k + quarter) >> 11
                angle = (k - (n << 11)).astype(F32) * F32(math.pi / PIX)
                sq = angle * angle
                c = -1 / 3628800
                for inv in (1 / 40320, -1 / 720, 1 / 24, -1 / 2, 1.0):
                    c = c * sq + F32(inv)
                d = 1 / 362880
                for inv in (-1 / 5040, 1 / 120, -1 / 6, 1.0):
                    d = d * sq + F32(inv)
                d = d * angle
                swap = (n & 1) == 1
                cosine = jnp.where(swap, d, c)
                sine = jnp.where(swap, c, d)
                cosine = jnp.where(((n + 1) & 2) == 2, -cosine, cosine)
                sine = jnp.where((n & 2) == 2, -sine, sine)
                for reim in range(2):
                    top = par * 128 + (2 * s + reim) * 32
                    for u in range(4):
                        turn = (mode[s] * u + reim) & 3
                        value = jnp.where((turn & 1) == 1, sine, cosine)
                        scale = jnp.where(((turn + 1) & 2) == 2, -gain[s], gain[s])
                        at = pl.ds(pl.multiple_of(u * quarter + first, 128), 128)
                        out_ref[top : top + 32, at] = (value * scale).astype(BF16)
        return carry

    lax.fori_loop(0, quarter // 128, chunk, 0)


def phase_table(m_values):
    return pl.pallas_call(
        table_kernel,
        out_shape=jax.ShapeDtypeStruct((256, PIX), BF16),
        in_specs=[pl.BlockSpec(memory_space=pltpu.SMEM)],
        out_specs=pl.BlockSpec(memory_space=pltpu.VMEM),
        cost_estimate=pl.CostEstimate(flops=8_000_000, bytes_accessed=2_097_152, transcendentals=0),
        name="phase_table",
    )(m_values)


def by_cycle(values, place):
    odd = jnp.zeros(place.shape, jnp.int32)
    for t in range(PER):
        odd = jnp.where(place == t, values[t], odd)
    return odd == 1


def pixel_kernel(ids_ref, x_ref, tab_ref, mix_ref, diag_ref, cross_ref, out_ref, rows_ref, acc_ref):
    fields = 2 * PAIRS
    parity = [ids_ref[t] & 1 for t in range(PER)]
    slot = iota((32, 128), 1) // 32
    rows_ref[...] = x_ref[...].astype(F32)
    per_cycle = [rows_ref[pl.ds(t, 32, stride=PER), :] for t in range(PER)]
    halves = []
    for high in range(2):
        blocks = []
        for sr in range(4):
            block = None
            for low in range(4):
                value = per_cycle[4 * high + low]
                shift = (low - sr) * 32 % 128
                value = pltpu.roll(value, shift, 1) if shift else value
                block = value if block is None else jnp.where(slot == low, value, block)
            blocks.append(block)
        halves.append(jnp.concatenate(blocks, 0))
    gathered = jnp.concatenate(halves, 1).astype(BF16)

    row, col = iota((fields * PER, 256), 0), iota((fields * PER, 256), 1)
    field = row // PER
    target = (row % PER) * 32 + field + jnp.where(field >= PAIRS, SLOT - PAIRS, 0)
    perm = jnp.where(col == target, 1.0, 0.0).astype(BF16)

    lhs = dot(perm, gathered, NT)
    odd_row = by_cycle(parity, iota(lhs.shape, 0) % PER)
    zero = jnp.zeros_like(lhs)
    lhs = jnp.concatenate(
        [jnp.where(odd_row, zero, lhs), jnp.where(odd_row, lhs, zero)], 1
    ).astype(BF16)

    width = 512
    for p in range(PIX // width):
        at = slice(p * width, (p + 1) * width)
        table = tab_ref[:, at]
        maps = dot(lhs, table, NN)
        mix = [mix_ref[0, c, :, at] for c in range(COMPS)]
        diag = [diag_ref[0, e, :, at] for e in range(2)]
        cross = cross_ref[0, :, at]
        back = [[None] * PAIRS, [None] * PAIRS]
        for chain in range(CHAINS):
            sky = []
            for e in range(2):
                total = None
                for c in range(COMPS):
                    f = e * PAIRS + chain * COMPS + c
                    part = maps[f * PER : (f + 1) * PER] * mix[c]
                    total = part if total is None else total + part
                sky.append(total)
            weighted = [
                diag[0] * sky[0] + cross * sky[1],
                cross * sky[0] + diag[1] * sky[1],
            ]
            for e in range(2):
                for c in range(COMPS):
                    back[e][chain * COMPS + c] = weighted[e] * mix[c]
        back = jnp.concatenate(back[0] + back[1], 0).astype(BF16)
        part = dot(table, back, NT)
        if p == 0:
            acc_ref[...] = part
        else:
            acc_ref[...] += part

    odd_lane = by_cycle(parity, iota((128, fields * PER), 1) % PER)
    returned = jnp.where(odd_lane, acc_ref[128:, :], acc_ref[:128, :]).astype(BF16)
    spread = dot(returned, perm, NN)
    for t in range(PER):
        high, low = divmod(t, 4)
        block = None
        for sr in range(4):
            value = spread[sr * 32 : (sr + 1) * 32, high * 128 : (high + 1) * 128]
            shift = (sr - low) * 32 % 128
            value = pltpu.roll(value, shift, 1) if shift else value
            block = value if block is None else jnp.where(slot == sr, value, block)
        rows_ref[pl.ds(t, 32, stride=PER), :] = block
    result = rows_ref[...].astype(BF16)
    out_ref[0] = result
    out_ref[1] = result


def pixels(cycle_ids, arrived, table, mixing, noise_diag, noise_cross):
    vmem = pl.BlockSpec(memory_space=pltpu.VMEM)
    return pl.pallas_call(
        pixel_kernel,
        out_shape=jax.ShapeDtypeStruct((2, 256, 128), BF16),
        in_specs=[pl.BlockSpec(memory_space=pltpu.SMEM)] + [vmem] * 5,
        out_specs=vmem,
        scratch_shapes=[pltpu.VMEM((256, 128), F32), pltpu.VMEM((256, 2 * PAIRS * PER), F32)],
        name="pixels",
    )(cycle_ids, arrived, table, mixing, noise_diag, noise_cross)


def adjoint_kernel(core_ref, r_ref, low_ref, high_ref, *rest):
    own_low, own_high, other_low, other_high, out_ref, lhs_ref, nat_ref = rest

    @pl.when(pl.program_id(0) == 0)
    def _():
        for b, index in enumerate((core_ref[0], 1 - core_ref[0])):
            turned = r_ref[index].astype(F32).T
            for s in range(2):
                rows = turned[s * 64 : (s + 1) * 64]
                slots = [rows[i * SLOT : (i + 1) * SLOT] for i in range(4)]
                at = slice(b * 64, (b + 1) * 64)
                lhs_ref[s, at, :256] = rows.astype(BF16)
                lhs_ref[s, at, 256:] = jnp.concatenate(crossed(slots), 0).astype(BF16)

    for half, tab_ref, own, other in (
        (0, low_ref, own_low, other_low),
        (1, high_ref, own_high, other_high),
    ):
        for s in range(2):
            sums = dot(lhs_ref[s, :, :256], tab_ref[s, 0], NN) + dot(
                lhs_ref[s, :, 256:], tab_ref[s, 1], NN
            )
            sums = sums[:64] * own[...] + sums[64:] * other[...]
            for i, place in enumerate(PLACE):
                nat_ref[half, s, pl.ds(place, SLOT, stride=4), :] = sums[i * SLOT : (i + 1) * SLOT]
            out_ref[half, 0, s] = nat_ref[half, s, :COLS, :].astype(BF16)


def adjoint(core, returned, tables, own_beam, other_beam):
    cycles = tables.shape[2]
    steps = 4

    def level(half):
        return lambda k, core: (0, 0, 0, 2 * (k + half * steps) + core[0])

    def beam_level(half):
        return lambda k, core: (0, 2 * (k + half * steps) + core[0])

    tab = [pl.BlockSpec((2, 2, cycles, 128), level(h)) for h in range(2)]
    beams = [pl.BlockSpec((1, 128), beam_level(h)) for h in range(2)]
    out = pl.pallas_call(
        adjoint_kernel,
        out_shape=jax.ShapeDtypeStruct((2, steps, 2, COLS, 128), BF16),
        grid_spec=pltpu.PrefetchScalarGridSpec(
            num_scalar_prefetch=1,
            grid=(steps,),
            in_specs=[pl.BlockSpec((2, cycles, 128), lambda k, core: (0, 0, 0))] + tab + beams * 2,
            out_specs=pl.BlockSpec((2, 1, 2, COLS, 128), lambda k, core: (0, k, 0, 0, 0)),
            scratch_shapes=[
                pltpu.VMEM((2, 128, 2 * cycles), BF16),
                pltpu.VMEM((2, 2, 64, 128), F32),
            ],
        ),
        name="adjoint",
    )(core, returned, tables, tables, own_beam, own_beam, other_beam, other_beam)
    return out.reshape(2 * steps, 2, COLS, 128)


def final_kernel(band_ref, sum_ref, coef_ref, prior_ref, out_ref):
    kind = iota((COLS, 128), 0) % (4 * COMPS) // 2
    prior = jnp.zeros((COLS, 128), F32)
    for k in range(2 * COMPS):
        prior = jnp.where(kind == k, prior_ref[k : k + 1, :], prior)
    for s in range(2):
        total = prior * coef_ref[s].astype(F32)
        for y in range(sum_ref.shape[0]):
            total = total + sum_ref[y, s].astype(F32)
        out_ref[s] = total


def final(band, gathered, coeffs_t, prior):
    return pl.pallas_call(
        final_kernel,
        out_shape=jax.ShapeDtypeStruct((2, COLS, 128), F32),
        grid_spec=pltpu.PrefetchScalarGridSpec(
            num_scalar_prefetch=1,
            grid=(1,),
            in_specs=[
                pl.BlockSpec(gathered.shape, lambda k, band: (0, 0, 0, 0)),
                pl.BlockSpec((2, COLS, 128), lambda k, band: (0, 0, band[0])),
                pl.BlockSpec((2 * COMPS, 128), lambda k, band: (0, 0)),
            ],
            out_specs=pl.BlockSpec((2, COLS, 128), lambda k, band: (0, 0, 0)),
        ),
        name="final",
    )(band, gathered, coeffs_t, prior)


def on_device(coeffs, tables, beam, mixing, noise_diag, noise_cross, prior, m_values, cycle_ids):
    core = lax.axis_index("core")
    band = (2 * lax.axis_index("y") + core).astype(jnp.int32)[None]
    core = core.astype(jnp.int32)[None]
    coeffs_t = coeffs.transpose(0, 2, 1)
    spectra = synth(coeffs_t, tables, beam)
    arrived = lax.all_to_all(spectra.reshape(32, PER, 128), "ma", 0, 0, tiled=True)
    table = phase_table(m_values)
    other_beam = lax.ppermute(beam, "core", [(0, 1), (1, 0)])
    returned = pixels(cycle_ids, arrived.reshape(256, 128), table, mixing, noise_diag, noise_cross)
    returned = lax.all_to_all(
        returned.reshape(64, PER, 128), ("core", "ma"), 0, 0, tiled=True
    ).reshape(2, 256, 128)
    partial = adjoint(core, returned, tables, beam, other_beam)
    gathered = lax.all_to_all(partial, "y", 0, 0, tiled=True)
    return final(band, gathered, coeffs_t, prior).transpose(0, 2, 1)


def solution(mesh):
    bands, modes = mesh.devices.shape
    fine = Mesh(mesh.devices.reshape(bands // 2, 2, modes), ("y", "core", "ma"))
    band = ("y", "core")
    in_specs = (
        P("ma", None, None),
        P("ma", None, None, None),
        P(band, None),
        P(band, None, "ma", None),
        P(band, None, "ma", None),
        P(band, "ma", None),
        P(None, band),
        P(),
        P("ma"),
    )
    return jax.shard_map(
        on_device, mesh=fine, in_specs=in_specs, out_specs=P("ma", band, None), check_vma=False
    )
```

```python
import math

import jax
import jax.numpy as jnp
from jax import lax
from jax.experimental import pallas as pl
from jax.experimental.pallas import tpu as pltpu
from jax.sharding import Mesh
from jax.sharding import PartitionSpec as P

F32 = jnp.float32
BF16 = jnp.bfloat16

PIX = 4096
COMPS = 3
CHAINS = 4
PAIRS = CHAINS * COMPS
COLS = 4 * PAIRS
SLOT = 16
PER = 8
PLACE = (0, 2, 1, 3)

NT = (((1,), (1,)), ((), ()))
NN = (((1,), (0,)), ((), ()))


def grant(mib):
    return pltpu.CompilerParams(vmem_limit_bytes=mib << 20)


def dot(a, b, dims):
    return lax.dot_general(a, b, dims, preferred_element_type=F32)


def crossed(slots):
    return [-slots[3], slots[2], slots[1], -slots[0]]


CHUNKS = 4


def synth_kernel(coef_hbm, tab_hbm, beam_hbm, out_ref, coef_ref, tab_ref, beam_ref, nat_ref, rows_ref, sems):
    levels = coef_ref.shape[2]
    width = levels // CHUNKS
    heads = [
        pltpu.make_async_copy(beam_hbm, beam_ref, sems.at[CHUNKS]),
        pltpu.make_async_copy(coef_hbm, coef_ref, sems.at[CHUNKS + 1]),
    ]
    for head in heads:
        head.start()
    copies = []
    for c in range(CHUNKS):
        at = pl.ds(c * width, width)
        copies.append(pltpu.make_async_copy(tab_hbm.at[:, :, :, at], tab_ref.at[c], sems.at[c]))
        copies[-1].start()
    nat_ref[...] = jnp.zeros_like(nat_ref)
    for head in heads:
        head.wait()
    for s in range(2):
        for j in range(levels // 128):
            at = slice(j * 128, (j + 1) * 128)
            beamed = (coef_ref[s, :, at].astype(F32) * beam_ref[:, at]).astype(BF16)
            nat_ref[s, j, :COLS, :] = beamed.astype(F32)
            slots = [nat_ref[s, j, pl.ds(p, SLOT, stride=4), :] for p in PLACE]
            for which, rows in enumerate((slots, crossed(slots))):
                rows_ref[s, which, :, at] = jnp.concatenate(rows, 0).astype(BF16)
    total = [None, None]
    for c in range(CHUNKS):
        copies[c].wait()
        for s in range(2):
            for which in range(2):
                rows = rows_ref[s, which, :, c * width : (c + 1) * width]
                part = dot(tab_ref[c, s, which], rows, NT)
                total[s] = part if total[s] is None else total[s] + part
    out_ref[...] = jnp.concatenate(total, 1).astype(BF16)


def synth(coeffs_t, tables, beam):
    _, cols, levels = coeffs_t.shape
    cycles = tables.shape[2]
    hbm = pl.BlockSpec(memory_space=pltpu.HBM)
    vmem = pl.BlockSpec(memory_space=pltpu.VMEM)
    return pl.pallas_call(
        synth_kernel,
        out_shape=jax.ShapeDtypeStruct((cycles, 128), BF16),
        in_specs=[hbm] * 3,
        out_specs=vmem,
        scratch_shapes=[
            pltpu.VMEM((2, cols, levels), BF16),
            pltpu.VMEM((CHUNKS, 2, 2, cycles, levels // CHUNKS), BF16),
            pltpu.VMEM((1, levels), F32),
            pltpu.VMEM((2, levels // 128, 4 * SLOT, 128), F32),
            pltpu.VMEM((2, 2, 4 * SLOT, levels), BF16),
            pltpu.SemaphoreType.DMA((CHUNKS + 2,)),
        ],
        compiler_params=grant(12),
        name="synth",
    )(coeffs_t, tables, beam)


def iota(shape, dim):
    return lax.broadcasted_iota(jnp.int32, shape, dim)


def table_kernel(m_ref, out_ref):
    quarter = PIX // 4
    row = iota((32, 128), 0)
    mode, gain = [], []
    for s in range(2):
        m = jnp.zeros((32, 128), jnp.int32)
        for j in range(32):
            m = jnp.where(row == j, m_ref[2 * j + s], m)
        mode.append(m)
        gain.append(jnp.where(m == 0, 1.0, 2.0).astype(F32))
    lane = iota((32, 128), 1)

    def chunk(i, carry):
        first = i * 128
        for par in range(2):
            for s in range(2):
                k = (mode[s] * (2 * (lane + first) + par)) & (2 * PIX - 1)
                n = (k + quarter) >> 11
                angle = (k - (n << 11)).astype(F32) * F32(math.pi / PIX)
                sq = angle * angle
                c = -1 / 3628800
                for inv in (1 / 40320, -1 / 720, 1 / 24, -1 / 2, 1.0):
                    c = c * sq + F32(inv)
                d = 1 / 362880
                for inv in (-1 / 5040, 1 / 120, -1 / 6, 1.0):
                    d = d * sq + F32(inv)
                d = d * angle
                swap = (n & 1) == 1
                cosine = jnp.where(swap, d, c)
                sine = jnp.where(swap, c, d)
                cosine = jnp.where(((n + 1) & 2) == 2, -cosine, cosine)
                sine = jnp.where((n & 2) == 2, -sine, sine)
                for reim in range(2):
                    top = par * 128 + (2 * s + reim) * 32
                    for u in range(4):
                        turn = (mode[s] * u + reim) & 3
                        value = jnp.where((turn & 1) == 1, sine, cosine)
                        scale = jnp.where(((turn + 1) & 2) == 2, -gain[s], gain[s])
                        at = pl.ds(pl.multiple_of(u * quarter + first, 128), 128)
                        out_ref[top : top + 32, at] = (value * scale).astype(BF16)
        return carry

    lax.fori_loop(0, quarter // 128, chunk, 0)


def phase_table(m_values):
    return pl.pallas_call(
        table_kernel,
        out_shape=jax.ShapeDtypeStruct((256, PIX), BF16),
        in_specs=[pl.BlockSpec(memory_space=pltpu.SMEM)],
        out_specs=pl.BlockSpec(memory_space=pltpu.VMEM),
        cost_estimate=pl.CostEstimate(flops=8_000_000, bytes_accessed=2_097_152, transcendentals=0),
        compiler_params=grant(6),
        name="phase_table",
    )(m_values)


def by_cycle(values, place):
    odd = jnp.zeros(place.shape, jnp.int32)
    for t in range(PER):
        odd = jnp.where(place == t, values[t], odd)
    return odd == 1


def pixel_kernel(ids_ref, x_ref, tab_ref, mix_ref, diag_ref, cross_ref, out_ref, rows_ref, acc_ref):
    fields = 2 * PAIRS
    parity = [ids_ref[t] & 1 for t in range(PER)]
    slot = iota((32, 128), 1) // 32
    rows_ref[...] = x_ref[...].astype(F32)
    per_cycle = [rows_ref[pl.ds(t, 32, stride=PER), :] for t in range(PER)]
    halves = []
    for high in range(2):
        blocks = []
        for sr in range(4):
            block = None
            for low in range(4):
                value = per_cycle[4 * high + low]
                shift = (low - sr) * 32 % 128
                value = pltpu.roll(value, shift, 1) if shift else value
                block = value if block is None else jnp.where(slot == low, value, block)
            blocks.append(block)
        halves.append(jnp.concatenate(blocks, 0))
    gathered = jnp.concatenate(halves, 1).astype(BF16)

    row, col = iota((fields * PER, 256), 0), iota((fields * PER, 256), 1)
    field = row // PER
    target = (row % PER) * 32 + field + jnp.where(field >= PAIRS, SLOT - PAIRS, 0)
    perm = jnp.where(col == target, 1.0, 0.0).astype(BF16)

    lhs = dot(perm, gathered, NT)
    odd_row = by_cycle(parity, iota(lhs.shape, 0) % PER)
    zero = jnp.zeros_like(lhs)
    lhs = jnp.concatenate(
        [jnp.where(odd_row, zero, lhs), jnp.where(odd_row, lhs, zero)], 1
    ).astype(BF16)

    width = 2048
    for p in range(PIX // width):
        at = slice(p * width, (p + 1) * width)
        table = tab_ref[:, at]
        maps = dot(lhs, table, NN)
        mix = [mix_ref[0, c, :, at] for c in range(COMPS)]
        diag = [diag_ref[0, e, :, at] for e in range(2)]
        cross = cross_ref[0, :, at]
        back = [[None] * PAIRS, [None] * PAIRS]
        for chain in range(CHAINS):
            sky = []
            for e in range(2):
                total = None
                for c in range(COMPS):
                    f = e * PAIRS + chain * COMPS + c
                    part = maps[f * PER : (f + 1) * PER] * mix[c]
                    total = part if total is None else total + part
                sky.append(total)
            weighted = [
                diag[0] * sky[0] + cross * sky[1],
                cross * sky[0] + diag[1] * sky[1],
            ]
            for e in range(2):
                for c in range(COMPS):
                    back[e][chain * COMPS + c] = weighted[e] * mix[c]
        back = jnp.concatenate(back[0] + back[1], 0).astype(BF16)
        part = dot(table, back, NT)
        if p == 0:
            acc_ref[...] = part
        else:
            acc_ref[...] += part

    odd_lane = by_cycle(parity, iota((128, fields * PER), 1) % PER)
    returned = jnp.where(odd_lane, acc_ref[128:, :], acc_ref[:128, :]).astype(BF16)
    spread = dot(returned, perm, NN)
    for t in range(PER):
        high, low = divmod(t, 4)
        block = None
        for sr in range(4):
            value = spread[sr * 32 : (sr + 1) * 32, high * 128 : (high + 1) * 128]
            shift = (sr - low) * 32 % 128
            value = pltpu.roll(value, shift, 1) if shift else value
            block = value if block is None else jnp.where(slot == sr, value, block)
        rows_ref[pl.ds(t, 32, stride=PER), :] = block
    result = rows_ref[...].astype(BF16)
    out_ref[0] = result
    out_ref[1] = result


def pixels(cycle_ids, arrived, table, mixing, noise_diag, noise_cross):
    vmem = pl.BlockSpec(memory_space=pltpu.VMEM)
    return pl.pallas_call(
        pixel_kernel,
        out_shape=jax.ShapeDtypeStruct((2, 256, 128), BF16),
        in_specs=[pl.BlockSpec(memory_space=pltpu.SMEM)] + [vmem] * 5,
        out_specs=vmem,
        scratch_shapes=[pltpu.VMEM((256, 128), F32), pltpu.VMEM((256, 2 * PAIRS * PER), F32)],
        compiler_params=grant(10),
        name="pixels",
    )(cycle_ids, arrived, table, mixing, noise_diag, noise_cross)


def fetch_kernel(core_ref, tab_hbm, beam_ref, out_ref, own_ref, sent_ref, sems):
    blocks = tab_hbm.shape[3] // 256
    copies = []
    for k in range(blocks):
        source = pl.ds(pl.multiple_of(256 * k + 128 * core_ref[0], 128), 128)
        place = pl.ds(128 * k, 128)
        copies.append(
            pltpu.make_async_copy(
                tab_hbm.at[:, :, :, source], out_ref.at[:, :, :, place], sems.at[k]
            )
        )
        copies[-1].start()
        pair = [beam_ref[:, (2 * k + c) * 128 : (2 * k + c + 1) * 128] for c in range(2)]
        second = core_ref[0] == 1
        own_ref[:, 128 * k : 128 * (k + 1)] = jnp.where(second, pair[1], pair[0])
        sent_ref[:, 128 * k : 128 * (k + 1)] = jnp.where(second, pair[0], pair[1])
    for copy in copies:
        copy.wait()


def fetch(core, tables, beam):
    levels = tables.shape[3]
    hbm = pl.BlockSpec(memory_space=pltpu.HBM)
    vmem = pl.BlockSpec(memory_space=pltpu.VMEM)
    return pl.pallas_call(
        fetch_kernel,
        out_shape=(
            jax.ShapeDtypeStruct(tables.shape[:3] + (levels // 2,), BF16),
            jax.ShapeDtypeStruct((1, levels // 2), F32),
            jax.ShapeDtypeStruct((1, levels // 2), F32),
        ),
        in_specs=[pl.BlockSpec(memory_space=pltpu.SMEM), hbm, vmem],
        out_specs=(vmem, vmem, vmem),
        scratch_shapes=[pltpu.SemaphoreType.DMA((levels // 256,))],
        compiler_params=grant(4),
        cost_estimate=pl.CostEstimate(flops=0, bytes_accessed=4_194_304, transcendentals=0),
        name="fetch",
    )(core, tables, beam)


def adjoint_kernel(core_ref, r_ref, tab_ref, own_ref, other_ref, out_ref, lhs_ref, nat_ref):
    cycles = tab_ref.shape[2]
    for b, index in enumerate((core_ref[0], 1 - core_ref[0])):
        turned = r_ref[index].astype(F32).T
        for s in range(2):
            rows = turned[s * 64 : (s + 1) * 64]
            slots = [rows[i * SLOT : (i + 1) * SLOT] for i in range(4)]
            at = slice(b * 64, (b + 1) * 64)
            lhs_ref[s, 0, at, :] = rows.astype(BF16)
            lhs_ref[s, 1, at, :] = jnp.concatenate(crossed(slots), 0).astype(BF16)

    width = 256
    for s in range(2):
        for k in range(tab_ref.shape[3] // width):
            at = slice(k * width, (k + 1) * width)
            sums = dot(lhs_ref[s, 0], tab_ref[s, 0, :, at], NN) + dot(
                lhs_ref[s, 1], tab_ref[s, 1, :, at], NN
            )
            sums = sums[:64] * own_ref[:, at] + sums[64:] * other_ref[:, at]
            for h in range(width // 128):
                y = k * (width // 128) + h
                for i, place in enumerate(PLACE):
                    part = sums[i * SLOT : (i + 1) * SLOT, h * 128 : (h + 1) * 128]
                    nat_ref[s, y, pl.ds(place, SLOT, stride=4), :] = part
                out_ref[y, s] = nat_ref[s, y, :COLS, :].astype(BF16)


def adjoint(core, returned, tables, own_beam, other_beam):
    cycles, levels = tables.shape[2:]
    blocks = levels // 128
    vmem = pl.BlockSpec(memory_space=pltpu.VMEM)
    return pl.pallas_call(
        adjoint_kernel,
        out_shape=jax.ShapeDtypeStruct((blocks, 2, COLS, 128), BF16),
        in_specs=[pl.BlockSpec(memory_space=pltpu.SMEM)] + [vmem] * 4,
        out_specs=vmem,
        scratch_shapes=[
            pltpu.VMEM((2, 2, 128, cycles), BF16),
            pltpu.VMEM((2, blocks, 64, 128), F32),
        ],
        compiler_params=grant(8),
        name="adjoint",
    )(core, returned, tables, own_beam, other_beam)


def final_kernel(band_ref, sum_ref, coef_ref, prior_ref, out_ref):
    kind = iota((COLS, 128), 0) % (4 * COMPS) // 2
    prior = jnp.zeros((COLS, 128), F32)
    for k in range(2 * COMPS):
        prior = jnp.where(kind == k, prior_ref[k : k + 1, :], prior)
    at = pl.ds(pl.multiple_of(128 * band_ref[0], 128), 128)
    for s in range(2):
        total = prior * coef_ref[s, :, at].astype(F32)
        for y in range(sum_ref.shape[0]):
            total = total + sum_ref[y, s].astype(F32)
        out_ref[s] = total


def final(band, gathered, coeffs_t, prior):
    vmem = pl.BlockSpec(memory_space=pltpu.VMEM)
    return pl.pallas_call(
        final_kernel,
        out_shape=jax.ShapeDtypeStruct((2, COLS, 128), F32),
        in_specs=[pl.BlockSpec(memory_space=pltpu.SMEM)] + [vmem] * 3,
        out_specs=vmem,
        compiler_params=grant(4),
        name="final",
    )(band, gathered, coeffs_t, prior)


def on_device(coeffs, tables, beam, mixing, noise_diag, noise_cross, prior, m_values, cycle_ids):
    core = lax.axis_index("core")
    band = (2 * lax.axis_index("y") + core).astype(jnp.int32)[None]
    core = core.astype(jnp.int32)[None]
    coeffs_t = coeffs.transpose(0, 2, 1)
    stored = pltpu.with_memory_space_constraint(tables, pltpu.HBM)
    spectra = synth(
        pltpu.with_memory_space_constraint(coeffs_t, pltpu.HBM),
        stored,
        pltpu.with_memory_space_constraint(beam, pltpu.HBM),
    )
    arrived = lax.all_to_all(spectra.reshape(32, PER, 128), "ma", 0, 0, tiled=True)
    table = phase_table(m_values)
    returned = pixels(cycle_ids, arrived.reshape(256, 128), table, mixing, noise_diag, noise_cross)
    returned = lax.all_to_all(
        returned.reshape(64, PER, 128), ("core", "ma"), 0, 0, tiled=True
    ).reshape(2, 256, 128)
    level_tables, own_beam, sent_beam = fetch(core, stored, beam)
    other_beam = lax.ppermute(sent_beam, "core", [(0, 1), (1, 0)])
    partial = adjoint(core, returned, level_tables, own_beam, other_beam)
    gathered = lax.all_to_all(partial, "y", 0, 0, tiled=True)
    return final(band, gathered, coeffs_t, prior).transpose(0, 2, 1)


def solution(mesh):
    bands, modes = mesh.devices.shape
    fine = Mesh(mesh.devices.reshape(bands // 2, 2, modes), ("y", "core", "ma"))
    band = ("y", "core")
    in_specs = (
        P("ma", None, None),
        P("ma", None, None, None),
        P(band, None),
        P(band, None, "ma", None),
        P(band, None, "ma", None),
        P(band, "ma", None),
        P(None, band),
        P(),
        P("ma"),
    )
    return jax.shard_map(
        on_device, mesh=fine, in_specs=in_specs, out_specs=P("ma", band, None), check_vma=False
    )
```

```python
import math

import jax
import jax.numpy as jnp
from jax import lax
from jax.experimental import pallas as pl
from jax.experimental.pallas import tpu as pltpu
from jax.sharding import Mesh
from jax.sharding import PartitionSpec as P

F32 = jnp.float32
BF16 = jnp.bfloat16

PIX = 4096
COMPS = 3
CHAINS = 4
PAIRS = CHAINS * COMPS
COLS = 4 * PAIRS
WIDE = 64
PER = 8

NT = (((1,), (1,)), ((), ()))
NN = (((1,), (0,)), ((), ()))


def grant(mib):
    return pltpu.CompilerParams(vmem_limit_bytes=mib << 20)


def iota(shape, dim):
    return lax.broadcasted_iota(jnp.int32, shape, dim)


def dot(a, b, dims):
    return lax.dot_general(a, b, dims, preferred_element_type=F32)


SIGN = (-1.0, 1.0, 1.0, -1.0)


CHUNKS = 4


def synth_kernel(
    coef_hbm, tab_hbm, beam_hbm, out_ref, coef_ref, tab_ref, beam_ref, rows_ref, nat_ref, cross_ref, sems
):
    levels = coef_ref.shape[2]
    width = levels // CHUNKS
    head = pltpu.make_async_copy(beam_hbm, beam_ref, sems.at[2, 0])
    head.start()
    copies = []
    for c in range(CHUNKS):
        at = pl.ds(c * width, width)
        copies.append(
            (
                pltpu.make_async_copy(coef_hbm.at[:, :, at], coef_ref.at[:, :, at], sems.at[0, c]),
                pltpu.make_async_copy(tab_hbm.at[:, :, :, at], tab_ref.at[c], sems.at[1, c]),
            )
        )
        for copy in copies[c]:
            copy.start()
    rows_ref[:, :, COLS:, :] = jnp.zeros_like(rows_ref[:, :, COLS:, :])
    head.wait()

    def prepare(c):
        copies[c][0].wait()
        for s in range(2):
            for j in range(c * width // 128, (c + 1) * width // 128):
                at = slice(j * 128, (j + 1) * 128)
                beamed = (coef_ref[s, :, at].astype(F32) * beam_ref[:, at]).astype(BF16)
                rows_ref[s, 0, :COLS, at] = beamed
                nat_ref[s, j] = beamed.astype(F32)
                for k in range(4):
                    value = nat_ref[s, j, pl.ds(3 - k, PAIRS, stride=4), :]
                    cross_ref[s, j, pl.ds(k, PAIRS, stride=4), :] = SIGN[k] * value
                rows_ref[s, 1, :COLS, at] = cross_ref[s, j].astype(BF16)

    prepare(0)
    total = [None, None]
    for c in range(CHUNKS):
        copies[c][1].wait()
        if c + 1 < CHUNKS:
            prepare(c + 1)
        for s in range(2):
            for which in range(2):
                rows = rows_ref[s, which, :, c * width : (c + 1) * width]
                part = dot(tab_ref[c, s, which], rows, NT)
                total[s] = part if total[s] is None else total[s] + part
    out_ref[...] = jnp.concatenate(total, 1).astype(BF16)


def synth(coeffs_t, tables, beam):
    _, cols, levels = coeffs_t.shape
    cycles = tables.shape[2]
    hbm = pl.BlockSpec(memory_space=pltpu.HBM)
    vmem = pl.BlockSpec(memory_space=pltpu.VMEM)
    return pl.pallas_call(
        synth_kernel,
        out_shape=jax.ShapeDtypeStruct((cycles, 128), BF16),
        in_specs=[hbm] * 3,
        out_specs=vmem,
        scratch_shapes=[
            pltpu.VMEM((2, cols, levels), BF16),
            pltpu.VMEM((CHUNKS, 2, 2, cycles, levels // CHUNKS), BF16),
            pltpu.VMEM((1, levels), F32),
            pltpu.VMEM((2, 2, WIDE, levels), BF16),
            pltpu.VMEM((2, levels // 128, COLS, 128), F32),
            pltpu.VMEM((2, levels // 128, COLS, 128), F32),
            pltpu.SemaphoreType.DMA((3, CHUNKS)),
        ],
        compiler_params=grant(12),
        name="synth",
    )(coeffs_t, tables, beam)


def table_kernel(m_ref, out_ref, perm_ref):
    row, col = iota(perm_ref.shape, 0), iota(perm_ref.shape, 1)
    field = row // PER
    upper = (field >= PAIRS).astype(jnp.int32)
    target = (row % PER) * (WIDE // 2) + 2 * (field - PAIRS * upper) + upper
    perm_ref[...] = jnp.where((col >> 1) == target, 1.0, 0.0).astype(BF16)

    quarter = PIX // 4
    row = iota((32, 128), 0)
    mode, gain = [], []
    for s in range(2):
        m = jnp.zeros((32, 128), jnp.int32)
        for j in range(32):
            m = jnp.where(row == j, m_ref[2 * j + s], m)
        mode.append(m)
        gain.append(jnp.where(m == 0, 1.0, 2.0).astype(F32))
    lane = iota((32, 128), 1)

    def chunk(i, carry):
        first = i * 128
        for par in range(2):
            for s in range(2):
                k = (mode[s] * (2 * (lane + first) + par)) & (2 * PIX - 1)
                n = (k + quarter) >> 11
                angle = (k - (n << 11)).astype(F32) * F32(math.pi / PIX)
                sq = angle * angle
                c = -1 / 3628800
                for inv in (1 / 40320, -1 / 720, 1 / 24, -1 / 2, 1.0):
                    c = c * sq + F32(inv)
                d = 1 / 362880
                for inv in (-1 / 5040, 1 / 120, -1 / 6, 1.0):
                    d = d * sq + F32(inv)
                d = d * angle
                swap = (n & 1) == 1
                cosine = jnp.where(swap, d, c)
                sine = jnp.where(swap, c, d)
                cosine = jnp.where(((n + 1) & 2) == 2, -cosine, cosine)
                sine = jnp.where((n & 2) == 2, -sine, sine)
                for reim in range(2):
                    top = par * 128 + (2 * reim + s) * 32
                    for u in range(4):
                        turn = (mode[s] * u + reim) & 3
                        value = jnp.where((turn & 1) == 1, sine, cosine)
                        scale = jnp.where(((turn + 1) & 2) == 2, -gain[s], gain[s])
                        at = pl.ds(pl.multiple_of(u * quarter + first, 128), 128)
                        out_ref[top : top + 32, at] = (value * scale).astype(BF16)
        return carry

    lax.fori_loop(0, quarter // 128, chunk, 0)


def phase_table(m_values):
    return pl.pallas_call(
        table_kernel,
        out_shape=(
            jax.ShapeDtypeStruct((256, PIX), BF16),
            jax.ShapeDtypeStruct((2 * PAIRS * PER, WIDE * PER), BF16),
        ),
        in_specs=[pl.BlockSpec(memory_space=pltpu.SMEM)],
        out_specs=[pl.BlockSpec(memory_space=pltpu.VMEM)] * 2,
        cost_estimate=pl.CostEstimate(flops=8_000_000, bytes_accessed=2_097_152, transcendentals=0),
        compiler_params=grant(6),
        name="phase_table",
    )(m_values)


def by_cycle(values, place):
    odd = jnp.zeros(place.shape, jnp.int32)
    for t in range(PER):
        odd = jnp.where(place == t, values[t], odd)
    return odd == 1


def pixel_kernel(
    ids_ref, x_ref, tab_ref, perm_ref, mix_ref, diag_ref, cross_ref, out_ref, rows_ref, acc_ref
):
    parity = [ids_ref[t] & 1 for t in range(PER)]
    lane = iota((32, 128), 1)
    left = lane < WIDE
    rows_ref[...] = x_ref[...].astype(F32)
    tiles = []
    for u in range(PER // 2):
        pair = [rows_ref[pl.ds(2 * u + i, 32, stride=PER), :] for i in range(2)]
        swapped = [pltpu.roll(v, WIDE, 1) for v in pair]
        modes = [jnp.where(left, pair[0], swapped[1]), jnp.where(left, swapped[0], pair[1])]
        tiles.append(
            jnp.concatenate(
                [jnp.where((lane & 1) == reim, v, 0.0) for reim in range(2) for v in modes], 0
            )
        )
    gathered = jnp.concatenate(tiles, 1).astype(BF16)

    lhs = dot(perm_ref[...], gathered, NT)
    odd_row = by_cycle(parity, iota(lhs.shape, 0) % PER)
    zero = jnp.zeros_like(lhs)
    lhs = jnp.concatenate(
        [jnp.where(odd_row, zero, lhs), jnp.where(odd_row, lhs, zero)], 1
    ).astype(BF16)

    width = 2048
    for p in range(PIX // width):
        at = slice(p * width, (p + 1) * width)
        table = tab_ref[:, at]
        maps = dot(lhs, table, NN)
        mix = [mix_ref[0, c, :, at] for c in range(COMPS)]
        diag = [diag_ref[0, e, :, at] for e in range(2)]
        cross = cross_ref[0, :, at]
        back = [[None] * PAIRS, [None] * PAIRS]
        for chain in range(CHAINS):
            sky = []
            for e in range(2):
                total = None
                for c in range(COMPS):
                    f = e * PAIRS + chain * COMPS + c
                    part = maps[f * PER : (f + 1) * PER] * mix[c]
                    total = part if total is None else total + part
                sky.append(total)
            weighted = [
                diag[0] * sky[0] + cross * sky[1],
                cross * sky[0] + diag[1] * sky[1],
            ]
            for e in range(2):
                for c in range(COMPS):
                    back[e][chain * COMPS + c] = weighted[e] * mix[c]
        back = jnp.concatenate(back[0] + back[1], 0).astype(BF16)
        part = dot(table, back, NT)
        if p == 0:
            acc_ref[...] = part
        else:
            acc_ref[...] += part

    odd_lane = by_cycle(parity, iota((128, acc_ref.shape[1]), 1) % PER)
    returned = jnp.where(odd_lane, acc_ref[128:, :], acc_ref[:128, :]).astype(BF16)
    spread = dot(returned, perm_ref[...], NN)
    for u in range(PER // 2):
        tile = spread[:, u * 128 : (u + 1) * 128]
        modes = [
            jnp.where((lane & 1) == 1, tile[64 + s * 32 : 96 + s * 32], tile[s * 32 : 32 + s * 32])
            for s in range(2)
        ]
        swapped = [pltpu.roll(v, WIDE, 1) for v in modes]
        rows_ref[pl.ds(2 * u, 32, stride=PER), :] = jnp.where(left, modes[0], swapped[1])
        rows_ref[pl.ds(2 * u + 1, 32, stride=PER), :] = jnp.where(left, swapped[0], modes[1])
    result = rows_ref[...].astype(BF16)
    out_ref[0] = result
    out_ref[1] = result


def pixels(cycle_ids, arrived, table, perm, mixing, noise_diag, noise_cross):
    vmem = pl.BlockSpec(memory_space=pltpu.VMEM)
    return pl.pallas_call(
        pixel_kernel,
        out_shape=jax.ShapeDtypeStruct((2, 256, 128), BF16),
        in_specs=[pl.BlockSpec(memory_space=pltpu.SMEM)] + [vmem] * 6,
        out_specs=vmem,
        scratch_shapes=[pltpu.VMEM((256, 128), F32), pltpu.VMEM((256, 2 * PAIRS * PER), F32)],
        compiler_params=grant(10),
        name="pixels",
    )(cycle_ids, arrived, table, perm, mixing, noise_diag, noise_cross)


def fetch_kernel(place_ref, tab_hbm, beam_ref, out_ref, own_ref, sent_ref, sems):
    blocks = tab_hbm.shape[3] // 256
    copies = []
    for k in range(blocks):
        source = pl.ds(pl.multiple_of(256 * k + 128 * place_ref[0], 128), 128)
        place = pl.ds(128 * k, 128)
        copies.append(
            pltpu.make_async_copy(
                tab_hbm.at[:, :, :, source], out_ref.at[:, :, :, place], sems.at[k]
            )
        )
        copies[-1].start()
        pair = [beam_ref[:, (2 * k + c) * 128 : (2 * k + c + 1) * 128] for c in range(2)]
        second = place_ref[0] == 1
        own_ref[:, 128 * k : 128 * (k + 1)] = jnp.where(second, pair[1], pair[0])
        sent_ref[:, 128 * k : 128 * (k + 1)] = jnp.where(second, pair[0], pair[1])
    for copy in copies:
        copy.wait()


def fetch(place, tables, beam):
    levels = tables.shape[3]
    hbm = pl.BlockSpec(memory_space=pltpu.HBM)
    vmem = pl.BlockSpec(memory_space=pltpu.VMEM)
    return pl.pallas_call(
        fetch_kernel,
        out_shape=(
            jax.ShapeDtypeStruct(tables.shape[:3] + (levels // 2,), BF16),
            jax.ShapeDtypeStruct((1, levels // 2), F32),
            jax.ShapeDtypeStruct((1, levels // 2), F32),
        ),
        in_specs=[pl.BlockSpec(memory_space=pltpu.SMEM), hbm, vmem],
        out_specs=(vmem, vmem, vmem),
        scratch_shapes=[pltpu.SemaphoreType.DMA((levels // 256,))],
        compiler_params=grant(4),
        cost_estimate=pl.CostEstimate(flops=0, bytes_accessed=4_194_304, transcendentals=0),
        name="fetch",
    )(place, tables, beam)


def adjoint_kernel(
    place_ref, r_ref, tab_ref, own_ref, other_ref, out_ref, lhs_ref, plain_ref, cross_ref
):
    for b, index in enumerate((place_ref[0], 1 - place_ref[0])):
        for h in range(2):
            half = slice(h * 128, (h + 1) * 128)
            plain_ref[b, h] = r_ref[index, half, :].astype(F32).T
            for k in range(4):
                value = plain_ref[b, h, pl.ds(3 - k, 32, stride=4), :]
                cross_ref[b, h, pl.ds(k, 32, stride=4), :] = SIGN[k] * value
            for s in range(2):
                at = slice(b * COLS, (b + 1) * COLS)
                rows = slice(s * WIDE, s * WIDE + COLS)
                lhs_ref[s, 0, at, half] = plain_ref[b, h, rows, :].astype(BF16)
                lhs_ref[s, 1, at, half] = cross_ref[b, h, rows, :].astype(BF16)

    width = 256
    for s in range(2):
        for k in range(tab_ref.shape[3] // width):
            at = slice(k * width, (k + 1) * width)
            sums = dot(lhs_ref[s, 0], tab_ref[s, 0, :, at], NN) + dot(
                lhs_ref[s, 1], tab_ref[s, 1, :, at], NN
            )
            sums = (sums[:COLS] * own_ref[:, at] + sums[COLS:] * other_ref[:, at]).astype(BF16)
            for h in range(width // 128):
                out_ref[k * (width // 128) + h, s] = sums[:, h * 128 : (h + 1) * 128]


def adjoint(place, returned, tables, own_beam, other_beam):
    cycles, levels = tables.shape[2:]
    blocks = levels // 128
    vmem = pl.BlockSpec(memory_space=pltpu.VMEM)
    return pl.pallas_call(
        adjoint_kernel,
        out_shape=jax.ShapeDtypeStruct((blocks, 2, COLS, 128), BF16),
        in_specs=[pl.BlockSpec(memory_space=pltpu.SMEM)] + [vmem] * 4,
        out_specs=vmem,
        scratch_shapes=[
            pltpu.VMEM((2, 2, 2 * COLS, cycles), BF16),
            pltpu.VMEM((2, 2, 128, 128), F32),
            pltpu.VMEM((2, 2, 128, 128), F32),
        ],
        compiler_params=grant(8),
        name="adjoint",
    )(place, returned, tables, own_beam, other_beam)


def final_kernel(place_ref, sum_ref, coef_ref, prior_ref, out_ref):
    kind = iota((COLS, 128), 0) % (4 * COMPS) // 2
    prior = jnp.zeros((COLS, 128), F32)
    for k in range(2 * COMPS):
        prior = jnp.where(kind == k, prior_ref[k : k + 1, :], prior)
    at = pl.ds(pl.multiple_of(128 * place_ref[1], 128), 128)
    for s in range(2):
        total = prior * coef_ref[s, :, at].astype(F32)
        for y in range(sum_ref.shape[0]):
            total = total + sum_ref[y, s].astype(F32)
        out_ref[s] = total


def final(place, gathered, coeffs_t, prior):
    vmem = pl.BlockSpec(memory_space=pltpu.VMEM)
    return pl.pallas_call(
        final_kernel,
        out_shape=jax.ShapeDtypeStruct((2, COLS, 128), F32),
        in_specs=[pl.BlockSpec(memory_space=pltpu.SMEM)] + [vmem] * 3,
        out_specs=vmem,
        compiler_params=grant(4),
        name="final",
    )(place, gathered, coeffs_t, prior)


def on_device(coeffs, tables, beam, mixing, noise_diag, noise_cross, prior, m_values, cycle_ids):
    core = lax.axis_index("core")
    place = jnp.stack([core, 2 * lax.axis_index("y") + core]).astype(jnp.int32)
    coeffs_t = coeffs.transpose(0, 2, 1)
    stored = pltpu.with_memory_space_constraint(tables, pltpu.HBM)
    spectra = synth(
        pltpu.with_memory_space_constraint(coeffs_t, pltpu.HBM),
        stored,
        pltpu.with_memory_space_constraint(beam, pltpu.HBM),
    )
    arrived = lax.all_to_all(spectra.reshape(32, PER, 128), "ma", 0, 0, tiled=True)
    table, perm = phase_table(m_values)
    returned = pixels(cycle_ids, arrived.reshape(256, 128), table, perm, mixing, noise_diag, noise_cross)
    returned = lax.all_to_all(
        returned.reshape(64, PER, 128), ("core", "ma"), 0, 0, tiled=True
    ).reshape(2, 256, 128)
    level_tables, own_beam, sent_beam = fetch(place, stored, beam)
    other_beam = lax.ppermute(sent_beam, "core", [(0, 1), (1, 0)])
    partial = adjoint(place, returned, level_tables, own_beam, other_beam)
    gathered = lax.all_to_all(partial, "y", 0, 0, tiled=True)
    return final(place, gathered, coeffs_t, prior).transpose(0, 2, 1)


def solution(mesh):
    bands, modes = mesh.devices.shape
    fine = Mesh(mesh.devices.reshape(bands // 2, 2, modes), ("y", "core", "ma"))
    band = ("y", "core")
    in_specs = (
        P("ma", None, None),
        P("ma", None, None, None),
        P(band, None),
        P(band, None, "ma", None),
        P(band, None, "ma", None),
        P(band, "ma", None),
        P(None, band),
        P(),
        P("ma"),
    )
    return jax.shard_map(
        on_device, mesh=fine, in_specs=in_specs, out_specs=P("ma", band, None), check_vma=False
    )
```

```python
import math

import jax
import jax.numpy as jnp
from jax import lax
from jax.experimental import pallas as pl
from jax.experimental.pallas import tpu as pltpu
from jax.sharding import Mesh
from jax.sharding import PartitionSpec as P

F32 = jnp.float32
BF16 = jnp.bfloat16

PIX = 4096
COMPS = 3
CHAINS = 4
PAIRS = CHAINS * COMPS
COLS = 4 * PAIRS
WIDE = 64
PER = 8

NT = (((1,), (1,)), ((), ()))
NN = (((1,), (0,)), ((), ()))


def grant(mib):
    return pltpu.CompilerParams(vmem_limit_bytes=mib << 20)


def iota(shape, dim):
    return lax.broadcasted_iota(jnp.int32, shape, dim)


def dot(a, b, dims):
    return lax.dot_general(a, b, dims, preferred_element_type=F32)


SIGN = (-1.0, 1.0, 1.0, -1.0)


CHUNKS = 8


def synth_kernel(coef_hbm, tab_hbm, beam_hbm, out_ref, coef_ref, tab_ref, beam_ref, rows_ref, nat_ref, cross_ref, sems):
    levels = coef_ref.shape[2]
    width = levels // CHUNKS
    heads = [
        pltpu.make_async_copy(beam_hbm, beam_ref, sems.at[CHUNKS]),
        pltpu.make_async_copy(coef_hbm, coef_ref, sems.at[CHUNKS + 1]),
    ]
    for head in heads:
        head.start()
    copies = []
    for c in range(CHUNKS):
        at = pl.ds(c * width, width)
        copies.append(pltpu.make_async_copy(tab_hbm.at[:, :, :, at], tab_ref.at[c], sems.at[c]))
        copies[-1].start()
    rows_ref[...] = jnp.zeros_like(rows_ref)
    for head in heads:
        head.wait()
    for s in range(2):
        for j in range(levels // 128):
            at = slice(j * 128, (j + 1) * 128)
            beamed = (coef_ref[s, :, at].astype(F32) * beam_ref[:, at]).astype(BF16)
            rows_ref[s, 0, 0:COLS, at] = beamed
            nat_ref[s, j, :COLS, :] = beamed.astype(F32)
            for k in range(4):
                value = nat_ref[s, j, pl.ds(3 - k, PAIRS, stride=4), :]
                cross_ref[s, j, pl.ds(k, PAIRS, stride=4), :] = SIGN[k] * value
            rows_ref[s, 1, 0:COLS, at] = cross_ref[s, j].astype(BF16)
    total = [None, None]
    for c in range(CHUNKS):
        copies[c].wait()
        for s in range(2):
            for which in range(2):
                rows = rows_ref[s, which, :, c * width : (c + 1) * width]
                part = dot(tab_ref[c, s, which], rows, NT)
                total[s] = part if total[s] is None else total[s] + part
    out = jnp.concatenate(total, 1)
    out_ref[...] = out.astype(BF16)


def synth(coeffs_t, tables, beam):
    _, cols, levels = coeffs_t.shape
    cycles = tables.shape[2]
    hbm = pl.BlockSpec(memory_space=pltpu.HBM)
    vmem = pl.BlockSpec(memory_space=pltpu.VMEM)
    return pl.pallas_call(
        synth_kernel,
        out_shape=jax.ShapeDtypeStruct((cycles, 128), BF16),
        in_specs=[hbm] * 3,
        out_specs=vmem,
        scratch_shapes=[
            pltpu.VMEM((2, cols, levels), BF16),
            pltpu.VMEM((CHUNKS, 2, 2, cycles, levels // CHUNKS), BF16),
            pltpu.VMEM((1, levels), F32),
            pltpu.VMEM((2, 2, WIDE, levels), BF16),
            pltpu.VMEM((2, levels // 128, COLS, 128), F32),
            pltpu.VMEM((2, levels // 128, COLS, 128), F32),
            pltpu.SemaphoreType.DMA((CHUNKS + 2,)),
        ],
        compiler_params=grant(12),
        name="synth",
    )(coeffs_t, tables, beam)


def odd_cycle(ids_ref, place):
    odd = jnp.zeros(place.shape, F32)
    for t in range(PER):
        odd = jnp.where(place == t, (ids_ref[t] & 1).astype(F32), odd)
    return odd


def table_kernel(m_ref, ids_ref, out_ref, perm_ref, odd_row_ref, odd_lane_ref):
    row, col = iota(perm_ref.shape, 0), iota(perm_ref.shape, 1)
    field = row // PER
    upper = (field >= PAIRS).astype(jnp.int32)
    target = (row % PER) * (WIDE // 2) + 2 * (field - PAIRS * upper) + upper
    perm_ref[...] = jnp.where((col >> 1) == target, 1.0, 0.0).astype(BF16)
    odd_row_ref[...] = odd_cycle(ids_ref, iota(odd_row_ref.shape, 0) % PER)
    odd_lane_ref[...] = odd_cycle(ids_ref, iota(odd_lane_ref.shape, 1) % PER)

    quarter = PIX // 4
    row = iota((32, 128), 0)
    mode, gain = [], []
    for s in range(2):
        m = jnp.zeros((32, 128), jnp.int32)
        for j in range(32):
            m = jnp.where(row == j, m_ref[2 * j + s], m)
        mode.append(m)
        gain.append(jnp.where(m == 0, 1.0, 2.0).astype(F32))
    lane = iota((32, 128), 1)

    def chunk(i, carry):
        first = i * 128
        for par in range(2):
            for s in range(2):
                k = (mode[s] * (2 * (lane + first) + par)) & (2 * PIX - 1)
                n = (k + quarter) >> 11
                angle = (k - (n << 11)).astype(F32) * F32(math.pi / PIX)
                sq = angle * angle
                c = -1 / 3628800
                for inv in (1 / 40320, -1 / 720, 1 / 24, -1 / 2, 1.0):
                    c = c * sq + F32(inv)
                d = 1 / 362880
                for inv in (-1 / 5040, 1 / 120, -1 / 6, 1.0):
                    d = d * sq + F32(inv)
                d = d * angle
                swap = (n & 1) == 1
                cosine = jnp.where(swap, d, c)
                sine = jnp.where(swap, c, d)
                cosine = jnp.where(((n + 1) & 2) == 2, -cosine, cosine)
                sine = jnp.where((n & 2) == 2, -sine, sine)
                for reim in range(2):
                    top = par * 128 + (2 * reim + s) * 32
                    for u in range(4):
                        turn = (mode[s] * u + reim) & 3
                        value = jnp.where((turn & 1) == 1, sine, cosine)
                        scale = jnp.where(((turn + 1) & 2) == 2, -gain[s], gain[s])
                        at = pl.ds(pl.multiple_of(u * quarter + first, 128), 128)
                        out_ref[top : top + 32, at] = (value * scale).astype(BF16)
        return carry

    lax.fori_loop(0, quarter // 128, chunk, 0)


def phase_table(m_values, cycle_ids):
    rows = 2 * PAIRS * PER
    return pl.pallas_call(
        table_kernel,
        out_shape=(
            jax.ShapeDtypeStruct((256, PIX), BF16),
            jax.ShapeDtypeStruct((rows, WIDE * PER), BF16),
            jax.ShapeDtypeStruct((rows, 128), F32),
            jax.ShapeDtypeStruct((8, rows), F32),
        ),
        in_specs=[pl.BlockSpec(memory_space=pltpu.SMEM)] * 2,
        out_specs=[pl.BlockSpec(memory_space=pltpu.VMEM)] * 4,
        cost_estimate=pl.CostEstimate(flops=8_000_000, bytes_accessed=2_097_152, transcendentals=0),
        compiler_params=grant(6),
        name="phase_table",
    )(m_values, cycle_ids)


def pixel_kernel(x_ref, tab_ref, perm_ref, odd_row_ref, odd_lane_ref, *rest):
    mix_ref, diag_ref, cross_ref, out_ref, rows_ref, acc_ref = rest
    lane = iota((32, 128), 1)
    left = lane < WIDE
    rows_ref[...] = x_ref[...].astype(F32)
    tiles = []
    for u in range(PER // 2):
        pair = [rows_ref[pl.ds(2 * u + i, 32, stride=PER), :] for i in range(2)]
        swapped = [pltpu.roll(v, WIDE, 1) for v in pair]
        modes = [jnp.where(left, pair[0], swapped[1]), jnp.where(left, swapped[0], pair[1])]
        tiles.append(
            jnp.concatenate(
                [jnp.where((lane & 1) == reim, v, 0.0) for reim in range(2) for v in modes], 0
            )
        )
    gathered = jnp.concatenate(tiles, 1).astype(BF16)

    lhs = dot(perm_ref[...], gathered, NT)
    odd_row = odd_row_ref[...] > 0.5
    zero = jnp.zeros_like(lhs)
    lhs = jnp.concatenate(
        [jnp.where(odd_row, zero, lhs), jnp.where(odd_row, lhs, zero)], 1
    ).astype(BF16)

    width = 4096
    for p in range(PIX // width):
        at = slice(p * width, (p + 1) * width)
        table = tab_ref[:, at]
        maps = dot(lhs, table, NN)
        mix = [mix_ref[0, c, :, at] for c in range(COMPS)]
        diag = [diag_ref[0, e, :, at] for e in range(2)]
        cross = cross_ref[0, :, at]
        back = [[None] * PAIRS, [None] * PAIRS]
        for chain in range(CHAINS):
            sky = []
            for e in range(2):
                total = None
                for c in range(COMPS):
                    f = e * PAIRS + chain * COMPS + c
                    part = maps[f * PER : (f + 1) * PER] * mix[c]
                    total = part if total is None else total + part
                sky.append(total)
            weighted = [
                diag[0] * sky[0] + cross * sky[1],
                cross * sky[0] + diag[1] * sky[1],
            ]
            for e in range(2):
                for c in range(COMPS):
                    back[e][chain * COMPS + c] = weighted[e] * mix[c]
        back = jnp.concatenate(back[0] + back[1], 0).astype(BF16)
        part = dot(table, back, NT)
        if p == 0:
            acc_ref[...] = part
        else:
            acc_ref[...] += part

    odd_lane = jnp.concatenate([odd_lane_ref[...]] * 16, 0) > 0.5
    returned = jnp.where(odd_lane, acc_ref[128:, :], acc_ref[:128, :]).astype(BF16)
    spread = dot(returned, perm_ref[...], NN)
    for u in range(PER // 2):
        tile = spread[:, u * 128 : (u + 1) * 128]
        modes = [
            jnp.where((lane & 1) == 1, tile[64 + s * 32 : 96 + s * 32], tile[s * 32 : 32 + s * 32])
            for s in range(2)
        ]
        swapped = [pltpu.roll(v, WIDE, 1) for v in modes]
        rows_ref[pl.ds(2 * u, 32, stride=PER), :] = jnp.where(left, modes[0], swapped[1])
        rows_ref[pl.ds(2 * u + 1, 32, stride=PER), :] = jnp.where(left, swapped[0], modes[1])
    result = rows_ref[...].astype(BF16)
    out_ref[0] = result
    out_ref[1] = result


def pixels(arrived, helpers, mixing, noise_diag, noise_cross):
    vmem = pl.BlockSpec(memory_space=pltpu.VMEM)
    return pl.pallas_call(
        pixel_kernel,
        out_shape=jax.ShapeDtypeStruct((2, 256, 128), BF16),
        in_specs=[vmem] * 8,
        out_specs=vmem,
        scratch_shapes=[pltpu.VMEM((256, 128), F32), pltpu.VMEM((256, 2 * PAIRS * PER), F32)],
        compiler_params=grant(10),
        name="pixels",
    )(arrived, *helpers, mixing, noise_diag, noise_cross)


def fetch_kernel(core_ref, band_ref, tab_hbm, beam_ref, out_ref, own_ref, sent_ref, sems):
    blocks = tab_hbm.shape[3] // 256
    copies = []
    for k in range(blocks):
        source = pl.ds(pl.multiple_of(256 * k + 128 * core_ref[0], 128), 128)
        place = pl.ds(128 * k, 128)
        copies.append(
            pltpu.make_async_copy(
                tab_hbm.at[:, :, :, source], out_ref.at[:, :, :, place], sems.at[k]
            )
        )
        copies[-1].start()
        pair = [beam_ref[:, (2 * k + c) * 128 : (2 * k + c + 1) * 128] for c in range(2)]
        second = core_ref[0] == 1
        own_ref[:, 128 * k : 128 * (k + 1)] = jnp.where(second, pair[1], pair[0])
        sent_ref[:, 128 * k : 128 * (k + 1)] = jnp.where(second, pair[0], pair[1])
    for copy in copies:
        copy.wait()


def fetch(core, band, tables, beam):
    levels = tables.shape[3]
    hbm = pl.BlockSpec(memory_space=pltpu.HBM)
    vmem = pl.BlockSpec(memory_space=pltpu.VMEM)
    return pl.pallas_call(
        fetch_kernel,
        out_shape=(
            jax.ShapeDtypeStruct(tables.shape[:3] + (levels // 2,), BF16),
            jax.ShapeDtypeStruct((1, levels // 2), F32),
            jax.ShapeDtypeStruct((1, levels // 2), F32),
        ),
        in_specs=[pl.BlockSpec(memory_space=pltpu.SMEM)] * 2 + [hbm, vmem],
        out_specs=(vmem, vmem, vmem),
        scratch_shapes=[pltpu.SemaphoreType.DMA((levels // 256,))],
        compiler_params=grant(4),
        cost_estimate=pl.CostEstimate(flops=0, bytes_accessed=4_194_304, transcendentals=0),
        name="fetch",
    )(core, band, tables, beam)


def adjoint_kernel(
    core_ref, r_ref, tab_ref, own_ref, other_ref, out_ref, lhs_ref, plain_ref, cross_ref
):
    for b, index in enumerate((core_ref[0], 1 - core_ref[0])):
        for h in range(2):
            half = slice(h * 128, (h + 1) * 128)
            plain_ref[b, h] = r_ref[index, half, :].astype(F32).T
            for k in range(4):
                value = plain_ref[b, h, pl.ds(3 - k, 32, stride=4), :]
                cross_ref[b, h, pl.ds(k, 32, stride=4), :] = SIGN[k] * value
            for s in range(2):
                at = slice(b * COLS, (b + 1) * COLS)
                rows = slice(s * WIDE, s * WIDE + COLS)
                lhs_ref[s, 0, at, half] = plain_ref[b, h, rows, :].astype(BF16)
                lhs_ref[s, 1, at, half] = cross_ref[b, h, rows, :].astype(BF16)

    width = 256
    for s in range(2):
        for k in range(tab_ref.shape[3] // width):
            at = slice(k * width, (k + 1) * width)
            sums = dot(lhs_ref[s, 0], tab_ref[s, 0, :, at], NN) + dot(
                lhs_ref[s, 1], tab_ref[s, 1, :, at], NN
            )
            sums = (sums[:COLS] * own_ref[:, at] + sums[COLS:] * other_ref[:, at]).astype(BF16)
            for h in range(width // 128):
                out_ref[k * (width // 128) + h, s] = sums[:, h * 128 : (h + 1) * 128]


def adjoint(core, returned, tables, own_beam, other_beam):
    cycles, levels = tables.shape[2:]
    blocks = levels // 128
    vmem = pl.BlockSpec(memory_space=pltpu.VMEM)
    return pl.pallas_call(
        adjoint_kernel,
        out_shape=jax.ShapeDtypeStruct((blocks, 2, COLS, 128), BF16),
        in_specs=[pl.BlockSpec(memory_space=pltpu.SMEM)] + [vmem] * 4,
        out_specs=vmem,
        scratch_shapes=[
            pltpu.VMEM((2, 2, 2 * COLS, cycles), BF16),
            pltpu.VMEM((2, 2, 128, 128), F32),
            pltpu.VMEM((2, 2, 128, 128), F32),
        ],
        compiler_params=grant(8),
        name="adjoint",
    )(core, returned, tables, own_beam, other_beam)


def final_kernel(band_ref, sum_ref, coef_ref, prior_ref, out_ref):
    kind = iota((COLS, 128), 0) % (4 * COMPS) // 2
    prior = jnp.zeros((COLS, 128), F32)
    for k in range(2 * COMPS):
        prior = jnp.where(kind == k, prior_ref[k : k + 1, :], prior)
    at = pl.ds(pl.multiple_of(128 * band_ref[0], 128), 128)
    for s in range(2):
        total = prior * coef_ref[s, :, at].astype(F32)
        for y in range(sum_ref.shape[0]):
            total = total + sum_ref[y, s].astype(F32)
        out_ref[s] = total


def final(band, gathered, coeffs_t, prior):
    vmem = pl.BlockSpec(memory_space=pltpu.VMEM)
    return pl.pallas_call(
        final_kernel,
        out_shape=jax.ShapeDtypeStruct((2, COLS, 128), F32),
        in_specs=[pl.BlockSpec(memory_space=pltpu.SMEM)] + [vmem] * 3,
        out_specs=vmem,
        compiler_params=grant(4),
        name="final",
    )(band, gathered, coeffs_t, prior)


def on_device(coeffs, tables, beam, mixing, noise_diag, noise_cross, prior, m_values, cycle_ids):
    core = lax.axis_index("core")
    band = (2 * lax.axis_index("y") + core).astype(jnp.int32)[None]
    core = core.astype(jnp.int32)[None]
    coeffs_t = coeffs.transpose(0, 2, 1)
    stored = pltpu.with_memory_space_constraint(tables, pltpu.HBM)
    spectra = synth(
        pltpu.with_memory_space_constraint(coeffs_t, pltpu.HBM),
        stored,
        pltpu.with_memory_space_constraint(beam, pltpu.HBM),
    )
    arrived = lax.all_to_all(spectra.reshape(32, PER, 128), "ma", 0, 0, tiled=True)
    helpers = phase_table(m_values, cycle_ids)
    returned = pixels(arrived.reshape(256, 128), helpers, mixing, noise_diag, noise_cross)
    returned = lax.all_to_all(
        returned.reshape(64, PER, 128), ("core", "ma"), 0, 0, tiled=True
    ).reshape(2, 256, 128)
    level_tables, own_beam, sent_beam = fetch(core, band, stored, beam)
    other_beam = lax.ppermute(sent_beam, "core", [(0, 1), (1, 0)])
    partial = adjoint(core, returned, level_tables, own_beam, other_beam)
    gathered = lax.all_to_all(partial, "y", 0, 0, tiled=True)
    return final(band, gathered, coeffs_t, prior).transpose(0, 2, 1)


def solution(mesh):
    bands, modes = mesh.devices.shape
    fine = Mesh(mesh.devices.reshape(bands // 2, 2, modes), ("y", "core", "ma"))
    band = ("y", "core")
    in_specs = (
        P("ma", None, None),
        P("ma", None, None, None),
        P(band, None),
        P(band, None, "ma", None),
        P(band, None, "ma", None),
        P(band, "ma", None),
        P(None, band),
        P(),
        P("ma"),
    )
    return jax.shard_map(
        on_device, mesh=fine, in_specs=in_specs, out_specs=P("ma", band, None), check_vma=False
    )
```

```python
import math

import jax
import jax.numpy as jnp
from jax import lax
from jax.experimental import pallas as pl
from jax.experimental.pallas import tpu as pltpu
from jax.sharding import Mesh
from jax.sharding import PartitionSpec as P

F32 = jnp.float32
BF16 = jnp.bfloat16

PIX = 4096
COMPS = 3
CHAINS = 4
PAIRS = CHAINS * COMPS
COLS = 4 * PAIRS
WIDE = 64
SPARE = WIDE - COLS
PER = 8

NT = (((1,), (1,)), ((), ()))
NN = (((1,), (0,)), ((), ()))


def grant(mib):
    return pltpu.CompilerParams(vmem_limit_bytes=mib << 20)


def iota(shape, dim):
    return lax.broadcasted_iota(jnp.int32, shape, dim)


def dot(a, b, dims):
    return lax.dot_general(a, b, dims, preferred_element_type=F32)


SIGN = (-1.0, 1.0, 1.0, -1.0)


CHUNKS = 4


def synth_kernel(coef_hbm, tab_hbm, beam_hbm, out_ref, coef_ref, tab_ref, beam_ref, rows_ref, nat_ref, cross_ref, sems):
    levels = coef_ref.shape[2]
    width = levels // CHUNKS
    heads = [
        pltpu.make_async_copy(beam_hbm, beam_ref, sems.at[CHUNKS]),
        pltpu.make_async_copy(coef_hbm, coef_ref, sems.at[CHUNKS + 1]),
    ]
    for head in heads:
        head.start()
    copies = []
    for c in range(CHUNKS):
        at = pl.ds(c * width, width)
        copies.append(pltpu.make_async_copy(tab_hbm.at[:, :, :, at], tab_ref.at[c], sems.at[c]))
        copies[-1].start()
    rows_ref[...] = jnp.zeros_like(rows_ref)
    for head in heads:
        head.wait()
    for s in range(2):
        for j in range(levels // 128):
            at = slice(j * 128, (j + 1) * 128)
            beamed = (coef_ref[s, :, at].astype(F32) * beam_ref[:, at]).astype(BF16)
            rows_ref[s, 0, 0:COLS, at] = beamed
            nat_ref[s, j, :COLS, :] = beamed.astype(F32)
            for k in range(4):
                value = nat_ref[s, j, pl.ds(3 - k, PAIRS, stride=4), :]
                cross_ref[s, j, pl.ds(k, PAIRS, stride=4), :] = SIGN[k] * value
            rows_ref[s, 1, 0:COLS, at] = cross_ref[s, j].astype(BF16)
    total = [None, None]
    for c in range(CHUNKS):
        copies[c].wait()
        for s in range(2):
            for which in range(2):
                rows = rows_ref[s, which, :, c * width : (c + 1) * width]
                part = dot(tab_ref[c, s, which], rows, NT)
                total[s] = part if total[s] is None else total[s] + part
    out = jnp.concatenate(total, 1)
    out_ref[...] = out.astype(BF16)


def synth(coeffs_t, tables, beam):
    _, cols, levels = coeffs_t.shape
    cycles = tables.shape[2]
    hbm = pl.BlockSpec(memory_space=pltpu.HBM)
    vmem = pl.BlockSpec(memory_space=pltpu.VMEM)
    return pl.pallas_call(
        synth_kernel,
        out_shape=jax.ShapeDtypeStruct((cycles, 128), BF16),
        in_specs=[hbm] * 3,
        out_specs=vmem,
        scratch_shapes=[
            pltpu.VMEM((2, cols, levels), BF16),
            pltpu.VMEM((CHUNKS, 2, 2, cycles, levels // CHUNKS), BF16),
            pltpu.VMEM((1, levels), F32),
            pltpu.VMEM((2, 2, WIDE, levels), BF16),
            pltpu.VMEM((2, levels // 128, COLS, 128), F32),
            pltpu.VMEM((2, levels // 128, COLS, 128), F32),
            pltpu.SemaphoreType.DMA((CHUNKS + 2,)),
        ],
        compiler_params=grant(12),
        name="synth",
    )(coeffs_t, tables, beam)


def odd_cycle(ids_ref, place):
    odd = jnp.zeros(place.shape, F32)
    for t in range(PER):
        odd = jnp.where(place == t, (ids_ref[t] & 1).astype(F32), odd)
    return odd


def beam_rows(part, row):
    lane, sub = iota((8, 128), 1), iota((8, 128), 0)
    value = jnp.broadcast_to(row, (8, 128))
    start = (part % 4) * 32
    first = pltpu.roll(value, (128 + COLS - start) % 128, 1)
    second = pltpu.roll(value, (128 + COLS + WIDE - SPARE - start) % 128, 1)
    value = jnp.where(lane < WIDE, first, second)
    value = jnp.where((lane & (WIDE - 1)) >= COLS, value, 0.0)
    high = value.astype(BF16).astype(F32)
    middle = (value - high).astype(BF16).astype(F32)
    low = value - high - middle
    return jnp.where(sub == 0, high, jnp.where(sub == 1, middle, jnp.where(sub == 2, low, 0.0)))


def table_kernel(m_ref, ids_ref, band_ref, part_ref, beam_ref, *outs):
    out_ref, perm_ref, odd_row_ref, odd_lane_ref, rows_ref = outs
    part = part_ref[0]
    for c in range(2):
        at = pl.ds(pl.multiple_of(256 * (part // 4) + 128 * c, 128), 128)
        rows_ref[c] = beam_rows(part, beam_ref[:, at])

    row, col = iota(perm_ref.shape, 0), iota(perm_ref.shape, 1)
    field = row // PER
    upper = (field >= PAIRS).astype(jnp.int32)
    target = (row % PER) * (WIDE // 2) + 2 * (field - PAIRS * upper) + upper
    perm_ref[...] = jnp.where((col >> 1) == target, 1.0, 0.0).astype(BF16)
    odd_row_ref[...] = odd_cycle(ids_ref, iota(odd_row_ref.shape, 0) % PER)
    odd_lane_ref[...] = odd_cycle(ids_ref, iota(odd_lane_ref.shape, 1) % PER)

    quarter = PIX // 4
    row = iota((32, 128), 0)
    mode, gain = [], []
    for s in range(2):
        m = jnp.zeros((32, 128), jnp.int32)
        for j in range(32):
            m = jnp.where(row == j, m_ref[2 * j + s], m)
        mode.append(m)
        gain.append(jnp.where(m == 0, 1.0, 2.0).astype(F32))
    lane = iota((32, 128), 1)

    def chunk(i, carry):
        first = i * 128
        for par in range(2):
            for s in range(2):
                k = (mode[s] * (2 * (lane + first) + par)) & (2 * PIX - 1)
                n = (k + quarter) >> 11
                angle = (k - (n << 11)).astype(F32) * F32(math.pi / PIX)
                sq = angle * angle
                c = -1 / 3628800
                for inv in (1 / 40320, -1 / 720, 1 / 24, -1 / 2, 1.0):
                    c = c * sq + F32(inv)
                d = 1 / 362880
                for inv in (-1 / 5040, 1 / 120, -1 / 6, 1.0):
                    d = d * sq + F32(inv)
                d = d * angle
                swap = (n & 1) == 1
                cosine = jnp.where(swap, d, c)
                sine = jnp.where(swap, c, d)
                cosine = jnp.where(((n + 1) & 2) == 2, -cosine, cosine)
                sine = jnp.where((n & 2) == 2, -sine, sine)
                for reim in range(2):
                    top = par * 128 + (2 * reim + s) * 32
                    for u in range(4):
                        turn = (mode[s] * u + reim) & 3
                        value = jnp.where((turn & 1) == 1, sine, cosine)
                        scale = jnp.where(((turn + 1) & 2) == 2, -gain[s], gain[s])
                        at = pl.ds(pl.multiple_of(u * quarter + first, 128), 128)
                        out_ref[top : top + 32, at] = (value * scale).astype(BF16)
        return carry

    lax.fori_loop(0, quarter // 128, chunk, 0)


def phase_table(m_values, cycle_ids, band, part, beam):
    rows = 2 * PAIRS * PER
    smem = pl.BlockSpec(memory_space=pltpu.SMEM)
    vmem = pl.BlockSpec(memory_space=pltpu.VMEM)
    return pl.pallas_call(
        table_kernel,
        out_shape=(
            jax.ShapeDtypeStruct((256, PIX), BF16),
            jax.ShapeDtypeStruct((rows, WIDE * PER), BF16),
            jax.ShapeDtypeStruct((rows, 128), F32),
            jax.ShapeDtypeStruct((8, rows), F32),
            jax.ShapeDtypeStruct((2, 8, 128), F32),
        ),
        in_specs=[smem] * 4 + [vmem],
        out_specs=[vmem] * 5,
        cost_estimate=pl.CostEstimate(flops=8_000_000, bytes_accessed=2_097_152, transcendentals=0),
        compiler_params=grant(6),
        name="phase_table",
    )(m_values, cycle_ids, band, part, beam)


def pixel_kernel(core_ref, x_ref, tab_ref, perm_ref, odd_row_ref, odd_lane_ref, beam_ref, *rest):
    mix_ref, diag_ref, cross_ref, levels_hbm, out_ref, levels_ref, rows_ref, acc_ref, sems = rest
    copies = []
    for k in range(levels_hbm.shape[3] // 256):
        source = pl.ds(pl.multiple_of(256 * k + 128 * core_ref[0], 128), 128)
        place = levels_ref.at[:, :, :, pl.ds(128 * k, 128)]
        copies.append(
            pltpu.make_async_copy(levels_hbm.at[:, :, :, source], place, sems.at[k])
        )
        copies[-1].start()
    lane = iota((32, 128), 1)
    left = lane < WIDE
    rows_ref[...] = x_ref[...].astype(F32)
    tiles = []
    for u in range(PER // 2):
        pair = [rows_ref[pl.ds(2 * u + i, 32, stride=PER), :] for i in range(2)]
        swapped = [pltpu.roll(v, WIDE, 1) for v in pair]
        modes = [jnp.where(left, pair[0], swapped[1]), jnp.where(left, swapped[0], pair[1])]
        tiles.append(
            jnp.concatenate(
                [jnp.where((lane & 1) == reim, v, 0.0) for reim in range(2) for v in modes], 0
            )
        )
    gathered = jnp.concatenate(tiles, 1).astype(BF16)

    lhs = dot(perm_ref[...], gathered, NT)
    odd_row = odd_row_ref[...] > 0.5
    zero = jnp.zeros_like(lhs)
    lhs = jnp.concatenate(
        [jnp.where(odd_row, zero, lhs), jnp.where(odd_row, lhs, zero)], 1
    ).astype(BF16)

    width = 4096
    for p in range(PIX // width):
        at = slice(p * width, (p + 1) * width)
        table = tab_ref[:, at]
        maps = dot(lhs, table, NN)
        mix = [mix_ref[0, c, :, at] for c in range(COMPS)]
        diag = [diag_ref[0, e, :, at] for e in range(2)]
        cross = cross_ref[0, :, at]
        back = [[None] * PAIRS, [None] * PAIRS]
        for chain in range(CHAINS):
            sky = []
            for e in range(2):
                total = None
                for c in range(COMPS):
                    f = e * PAIRS + chain * COMPS + c
                    part = maps[f * PER : (f + 1) * PER] * mix[c]
                    total = part if total is None else total + part
                sky.append(total)
            weighted = [
                diag[0] * sky[0] + cross * sky[1],
                cross * sky[0] + diag[1] * sky[1],
            ]
            for e in range(2):
                for c in range(COMPS):
                    back[e][chain * COMPS + c] = weighted[e] * mix[c]
        back = jnp.concatenate(back[0] + back[1], 0).astype(BF16)
        part = dot(table, back, NT)
        if p == 0:
            acc_ref[...] = part
        else:
            acc_ref[...] += part

    odd_lane = jnp.concatenate([odd_lane_ref[...]] * 16, 0) > 0.5
    returned = jnp.where(odd_lane, acc_ref[128:, :], acc_ref[:128, :]).astype(BF16)
    spread = dot(returned, perm_ref[...], NN)
    for u in range(PER // 2):
        tile = spread[:, u * 128 : (u + 1) * 128]
        modes = [
            jnp.where((lane & 1) == 1, tile[64 + s * 32 : 96 + s * 32], tile[s * 32 : 32 + s * 32])
            for s in range(2)
        ]
        swapped = [pltpu.roll(v, WIDE, 1) for v in modes]
        rows_ref[pl.ds(2 * u, 32, stride=PER), :] = jnp.where(left, modes[0], swapped[1])
        rows_ref[pl.ds(2 * u + 1, 32, stride=PER), :] = jnp.where(left, swapped[0], modes[1])
    result = rows_ref[...].reshape(32, PER, 128)
    for c in range(2):
        out_ref[c] = (result + beam_ref[c][None]).reshape(256, 128).astype(BF16)
    for copy in copies:
        copy.wait()


def pixels(core, arrived, helpers, mixing, noise_diag, noise_cross, tables):
    levels = tables.shape[3] // 2
    vmem = pl.BlockSpec(memory_space=pltpu.VMEM)
    smem = pl.BlockSpec(memory_space=pltpu.SMEM)
    return pl.pallas_call(
        pixel_kernel,
        out_shape=(
            jax.ShapeDtypeStruct((2, 256, 128), BF16),
            jax.ShapeDtypeStruct(tables.shape[:3] + (levels,), BF16),
        ),
        in_specs=[smem] + [vmem] * 9 + [pl.BlockSpec(memory_space=pltpu.HBM)],
        out_specs=(vmem, vmem),
        scratch_shapes=[
            pltpu.VMEM((256, 128), F32),
            pltpu.VMEM((256, 2 * PAIRS * PER), F32),
            pltpu.SemaphoreType.DMA((levels // 128,)),
        ],
        compiler_params=grant(10),
        name="pixels",
    )(core, arrived, *helpers, mixing, noise_diag, noise_cross, tables)


def gather_beam(stage_ref, beam_ref):
    parts = [stage_ref[pl.ds(i, 32, stride=PER), :] for i in range(3)]
    stage_ref[:32, :] = parts[0] + parts[1] + parts[2]
    lane = iota((8, 128), 1)
    total = jnp.zeros((8, 128), F32)
    for m in range(4):
        value = stage_ref[pl.ds(m, 8, stride=4), :]
        for i in range(2):
            source, place = COLS + i * WIDE, m * 32 + i * SPARE
            shift = (place - source) % 128
            moved = pltpu.roll(value, shift, 1) if shift else value
            total = jnp.where((lane >= place) & (lane < place + SPARE), moved, total)
    beam_ref[...] = total


def adjoint_kernel(
    core_ref, r_ref, tab_ref, out_ref, lhs_ref, plain_ref, cross_ref, stage_ref, beam_ref
):
    for b, index in enumerate((core_ref[0], 1 - core_ref[0])):
        stage_ref[b] = r_ref[index].astype(F32)
        for h in range(2):
            half = slice(h * 128, (h + 1) * 128)
            plain_ref[b, h] = stage_ref[b, half, :].T
            for k in range(4):
                value = plain_ref[b, h, pl.ds(3 - k, 32, stride=4), :]
                cross_ref[b, h, pl.ds(k, 32, stride=4), :] = SIGN[k] * value
            for s in range(2):
                at = slice(b * COLS, (b + 1) * COLS)
                rows = slice(s * WIDE, s * WIDE + COLS)
                lhs_ref[s, 0, at, half] = plain_ref[b, h, rows, :].astype(BF16)
                lhs_ref[s, 1, at, half] = cross_ref[b, h, rows, :].astype(BF16)
        gather_beam(stage_ref.at[b], beam_ref.at[b])

    width = 256
    for s in range(2):
        for k in range(tab_ref.shape[3] // width):
            at = slice(k * width, (k + 1) * width)
            sums = dot(lhs_ref[s, 0], tab_ref[s, 0, :, at], NN) + dot(
                lhs_ref[s, 1], tab_ref[s, 1, :, at], NN
            )
            for h in range(2):
                y = 2 * k + h
                part = sums[:, h * 128 : (h + 1) * 128]
                part = part[:COLS] * beam_ref[0, y : y + 1, :] + part[COLS:] * beam_ref[1, y : y + 1, :]
                out_ref[y, s] = part.astype(BF16)


def adjoint(core, returned, tables):
    cycles, levels = tables.shape[2:]
    blocks = levels // 128
    vmem = pl.BlockSpec(memory_space=pltpu.VMEM)
    return pl.pallas_call(
        adjoint_kernel,
        out_shape=jax.ShapeDtypeStruct((blocks, 2, COLS, 128), BF16),
        in_specs=[pl.BlockSpec(memory_space=pltpu.SMEM)] + [vmem] * 2,
        out_specs=vmem,
        scratch_shapes=[
            pltpu.VMEM((2, 2, 2 * COLS, cycles), BF16),
            pltpu.VMEM((2, 2, 128, 128), F32),
            pltpu.VMEM((2, 2, 128, 128), F32),
            pltpu.VMEM((2, cycles, 128), F32),
            pltpu.VMEM((2, blocks, 128), F32),
        ],
        compiler_params=grant(8),
        name="adjoint",
    )(core, returned, tables)


def final_kernel(band_ref, sum_ref, coef_ref, prior_ref, out_ref):
    kind = iota((COLS, 128), 0) % (4 * COMPS) // 2
    prior = jnp.zeros((COLS, 128), F32)
    for k in range(2 * COMPS):
        prior = jnp.where(kind == k, prior_ref[k : k + 1, :], prior)
    at = pl.ds(pl.multiple_of(128 * band_ref[0], 128), 128)
    for s in range(2):
        total = prior * coef_ref[s, :, at].astype(F32)
        for y in range(sum_ref.shape[0]):
            total = total + sum_ref[y, s].astype(F32)
        out_ref[s] = total


def final(band, gathered, coeffs_t, prior):
    vmem = pl.BlockSpec(memory_space=pltpu.VMEM)
    return pl.pallas_call(
        final_kernel,
        out_shape=jax.ShapeDtypeStruct((2, COLS, 128), F32),
        in_specs=[pl.BlockSpec(memory_space=pltpu.SMEM)] + [vmem] * 3,
        out_specs=vmem,
        compiler_params=grant(4),
        name="final",
    )(band, gathered, coeffs_t, prior)


def on_device(coeffs, tables, beam, mixing, noise_diag, noise_cross, prior, m_values, cycle_ids):
    core = lax.axis_index("core")
    band = (2 * lax.axis_index("y") + core).astype(jnp.int32)[None]
    core = core.astype(jnp.int32)[None]
    coeffs_t = coeffs.transpose(0, 2, 1)
    stored = pltpu.with_memory_space_constraint(tables, pltpu.HBM)
    spectra = synth(
        pltpu.with_memory_space_constraint(coeffs_t, pltpu.HBM),
        stored,
        pltpu.with_memory_space_constraint(beam, pltpu.HBM),
    )
    arrived = lax.all_to_all(spectra.reshape(32, PER, 128), "ma", 0, 0, tiled=True)
    part = lax.axis_index("ma").astype(jnp.int32)[None]
    helpers = phase_table(m_values, cycle_ids, band, part, beam)
    arrived = arrived.reshape(256, 128)
    returned, level_tables = pixels(
        core, arrived, helpers, mixing, noise_diag, noise_cross, stored
    )
    returned = lax.all_to_all(
        returned.reshape(64, PER, 128), ("core", "ma"), 0, 0, tiled=True
    ).reshape(2, 256, 128)
    partial = adjoint(core, returned, level_tables)
    gathered = lax.all_to_all(partial, "y", 0, 0, tiled=True)
    return final(band, gathered, coeffs_t, prior).transpose(0, 2, 1)


def solution(mesh):
    bands, modes = mesh.devices.shape
    fine = Mesh(mesh.devices.reshape(bands // 2, 2, modes), ("y", "core", "ma"))
    band = ("y", "core")
    in_specs = (
        P("ma", None, None),
        P("ma", None, None, None),
        P(band, None),
        P(band, None, "ma", None),
        P(band, None, "ma", None),
        P(band, "ma", None),
        P(None, band),
        P(),
        P("ma"),
    )
    return jax.shard_map(
        on_device, mesh=fine, in_specs=in_specs, out_specs=P("ma", band, None), check_vma=False
    )
```

```python
import math

import jax
import jax.numpy as jnp
from jax import lax
from jax.experimental import pallas as pl
from jax.experimental.pallas import tpu as pltpu
from jax.sharding import Mesh
from jax.sharding import PartitionSpec as P

F32 = jnp.float32
BF16 = jnp.bfloat16

PIX = 4096
COMPS = 3
CHAINS = 4
PAIRS = CHAINS * COMPS
COLS = 4 * PAIRS
WIDE = 64
SPARE = WIDE - COLS
PER = 8

NT = (((1,), (1,)), ((), ()))
NN = (((1,), (0,)), ((), ()))


def grant(mib):
    return pltpu.CompilerParams(vmem_limit_bytes=mib << 20)


def iota(shape, dim):
    return lax.broadcasted_iota(jnp.int32, shape, dim)


def dot(a, b, dims):
    return lax.dot_general(a, b, dims, preferred_element_type=F32)


SIGN = (-1.0, 1.0, 1.0, -1.0)


CHUNKS = 4


def synth_kernel(coef_hbm, tab_hbm, beam_hbm, out_ref, coef_ref, tab_ref, beam_ref, rows_ref, nat_ref, cross_ref, sems):
    levels = coef_ref.shape[2]
    width = levels // CHUNKS
    heads = [
        pltpu.make_async_copy(beam_hbm, beam_ref, sems.at[CHUNKS]),
        pltpu.make_async_copy(coef_hbm, coef_ref, sems.at[CHUNKS + 1]),
    ]
    for head in heads:
        head.start()
    copies = []
    for c in range(CHUNKS):
        at = pl.ds(c * width, width)
        copies.append(pltpu.make_async_copy(tab_hbm.at[:, :, :, at], tab_ref.at[c], sems.at[c]))
        copies[-1].start()
    rows_ref[...] = jnp.zeros_like(rows_ref)
    for head in heads:
        head.wait()
    for s in range(2):
        for j in range(levels // 128):
            at = slice(j * 128, (j + 1) * 128)
            beamed = (coef_ref[s, :, at].astype(F32) * beam_ref[:, at]).astype(BF16)
            rows_ref[s, 0, 0:COLS, at] = beamed
            nat_ref[s, j, :COLS, :] = beamed.astype(F32)
            for k in range(4):
                value = nat_ref[s, j, pl.ds(3 - k, PAIRS, stride=4), :]
                cross_ref[s, j, pl.ds(k, PAIRS, stride=4), :] = SIGN[k] * value
            rows_ref[s, 1, 0:COLS, at] = cross_ref[s, j].astype(BF16)
    total = [None, None]
    for c in range(CHUNKS):
        copies[c].wait()
        for s in range(2):
            for which in range(2):
                rows = rows_ref[s, which, :, c * width : (c + 1) * width]
                part = dot(tab_ref[c, s, which], rows, NT)
                total[s] = part if total[s] is None else total[s] + part
    out = jnp.concatenate(total, 1)
    out_ref[...] = out.astype(BF16)


def synth(coeffs_t, tables, beam):
    _, cols, levels = coeffs_t.shape
    cycles = tables.shape[2]
    hbm = pl.BlockSpec(memory_space=pltpu.HBM)
    vmem = pl.BlockSpec(memory_space=pltpu.VMEM)
    return pl.pallas_call(
        synth_kernel,
        out_shape=jax.ShapeDtypeStruct((cycles, 128), BF16),
        in_specs=[hbm] * 3,
        out_specs=vmem,
        scratch_shapes=[
            pltpu.VMEM((2, cols, levels), BF16),
            pltpu.VMEM((CHUNKS, 2, 2, cycles, levels // CHUNKS), BF16),
            pltpu.VMEM((1, levels), F32),
            pltpu.VMEM((2, 2, WIDE, levels), BF16),
            pltpu.VMEM((2, levels // 128, COLS, 128), F32),
            pltpu.VMEM((2, levels // 128, COLS, 128), F32),
            pltpu.SemaphoreType.DMA((CHUNKS + 2,)),
        ],
        compiler_params=grant(12),
        name="synth",
    )(coeffs_t, tables, beam)


def odd_cycle(ids_ref, place):
    odd = jnp.zeros(place.shape, F32)
    for t in range(PER):
        odd = jnp.where(place == t, (ids_ref[t] & 1).astype(F32), odd)
    return odd


def beam_rows(part, row):
    lane, sub = iota((8, 128), 1), iota((8, 128), 0)
    value = jnp.broadcast_to(row, (8, 128))
    start = (part % 4) * 32
    first = pltpu.roll(value, (128 + COLS - start) % 128, 1)
    second = pltpu.roll(value, (128 + COLS + WIDE - SPARE - start) % 128, 1)
    value = jnp.where(lane < WIDE, first, second)
    value = jnp.where((lane & (WIDE - 1)) >= COLS, value, 0.0)
    high = value.astype(BF16).astype(F32)
    middle = (value - high).astype(BF16).astype(F32)
    low = value - high - middle
    return jnp.where(sub == 0, high, jnp.where(sub == 1, middle, jnp.where(sub == 2, low, 0.0)))


def table_kernel(m_ref, ids_ref, core_ref, band_ref, part_ref, beam_ref, levels_hbm, *rest):
    out_ref, perm_ref, odd_row_ref, odd_lane_ref, rows_ref, compact_hbm, held_ref, sems = rest
    inward, outward = [], []
    for k in range(levels_hbm.shape[3] // 256):
        source = pl.ds(pl.multiple_of(256 * k + 128 * core_ref[0], 128), 128)
        place = pl.ds(128 * k, 128)
        held = held_ref.at[:, :, :, place]
        inward.append(
            pltpu.make_async_copy(levels_hbm.at[:, :, :, source], held, sems.at[0, k])
        )
        outward.append(
            pltpu.make_async_copy(held, compact_hbm.at[:, :, :, place], sems.at[1, k])
        )
        inward[-1].start()
    part = part_ref[0]
    for c in range(2):
        at = pl.ds(pl.multiple_of(256 * (part // 4) + 128 * c, 128), 128)
        rows_ref[c] = beam_rows(part, beam_ref[:, at])

    row, col = iota(perm_ref.shape, 0), iota(perm_ref.shape, 1)
    field = row // PER
    upper = (field >= PAIRS).astype(jnp.int32)
    target = (row % PER) * (WIDE // 2) + 2 * (field - PAIRS * upper) + upper
    perm_ref[...] = jnp.where((col >> 1) == target, 1.0, 0.0).astype(BF16)
    odd_row_ref[...] = odd_cycle(ids_ref, iota(odd_row_ref.shape, 0) % PER)
    odd_lane_ref[...] = odd_cycle(ids_ref, iota(odd_lane_ref.shape, 1) % PER)

    quarter = PIX // 4
    row = iota((32, 128), 0)
    mode, gain = [], []
    for s in range(2):
        m = jnp.zeros((32, 128), jnp.int32)
        for j in range(32):
            m = jnp.where(row == j, m_ref[2 * j + s], m)
        mode.append(m)
        gain.append(jnp.where(m == 0, 1.0, 2.0).astype(F32))
    lane = iota((32, 128), 1)

    def chunk(i, carry):
        first = i * 128
        for par in range(2):
            for s in range(2):
                k = (mode[s] * (2 * (lane + first) + par)) & (2 * PIX - 1)
                n = (k + quarter) >> 11
                angle = (k - (n << 11)).astype(F32) * F32(math.pi / PIX)
                sq = angle * angle
                c = -1 / 3628800
                for inv in (1 / 40320, -1 / 720, 1 / 24, -1 / 2, 1.0):
                    c = c * sq + F32(inv)
                d = 1 / 362880
                for inv in (-1 / 5040, 1 / 120, -1 / 6, 1.0):
                    d = d * sq + F32(inv)
                d = d * angle
                swap = (n & 1) == 1
                cosine = jnp.where(swap, d, c)
                sine = jnp.where(swap, c, d)
                cosine = jnp.where(((n + 1) & 2) == 2, -cosine, cosine)
                sine = jnp.where((n & 2) == 2, -sine, sine)
                for reim in range(2):
                    top = par * 128 + (2 * reim + s) * 32
                    for u in range(4):
                        turn = (mode[s] * u + reim) & 3
                        value = jnp.where((turn & 1) == 1, sine, cosine)
                        scale = jnp.where(((turn + 1) & 2) == 2, -gain[s], gain[s])
                        at = pl.ds(pl.multiple_of(u * quarter + first, 128), 128)
                        out_ref[top : top + 32, at] = (value * scale).astype(BF16)
        return carry

    lax.fori_loop(0, quarter // 256, chunk, 0)
    for k in range(len(inward)):
        inward[k].wait()
        outward[k].start()
    lax.fori_loop(quarter // 256, quarter // 128, chunk, 0)
    for copy in outward:
        copy.wait()


def phase_table(m_values, cycle_ids, core, band, part, beam, tables):
    rows = 2 * PAIRS * PER
    compact = tables.shape[:3] + (tables.shape[3] // 2,)
    smem = pl.BlockSpec(memory_space=pltpu.SMEM)
    vmem = pl.BlockSpec(memory_space=pltpu.VMEM)
    return pl.pallas_call(
        table_kernel,
        out_shape=(
            jax.ShapeDtypeStruct((256, PIX), BF16),
            jax.ShapeDtypeStruct((rows, WIDE * PER), BF16),
            jax.ShapeDtypeStruct((rows, 128), F32),
            jax.ShapeDtypeStruct((8, rows), F32),
            jax.ShapeDtypeStruct((2, 8, 128), F32),
            pltpu.HBM(compact, BF16),
        ),
        in_specs=[smem] * 5 + [vmem, pl.BlockSpec(memory_space=pltpu.HBM)],
        out_specs=[vmem] * 5 + [pl.BlockSpec(memory_space=pltpu.HBM)],
        scratch_shapes=[pltpu.VMEM(compact, BF16), pltpu.SemaphoreType.DMA((2, compact[3] // 128))],
        cost_estimate=pl.CostEstimate(flops=8_000_000, bytes_accessed=2_097_152, transcendentals=0),
        compiler_params=grant(8),
        name="phase_table",
    )(m_values, cycle_ids, core, band, part, beam, tables)


def pixel_kernel(x_ref, tab_ref, perm_ref, odd_row_ref, odd_lane_ref, beam_ref, *rest):
    mix_ref, diag_ref, cross_ref, compact_hbm, out_ref, levels_ref, rows_ref, acc_ref, sems = rest
    copies = []
    for k in range(CHUNKS):
        at = pl.ds(k * compact_hbm.shape[3] // CHUNKS, compact_hbm.shape[3] // CHUNKS)
        source, place = compact_hbm.at[:, :, :, at], levels_ref.at[:, :, :, at]
        copies.append(pltpu.make_async_copy(source, place, sems.at[k]))
        copies[-1].start()
    lane = iota((32, 128), 1)
    left = lane < WIDE
    rows_ref[...] = x_ref[...].astype(F32)
    tiles = []
    for u in range(PER // 2):
        pair = [rows_ref[pl.ds(2 * u + i, 32, stride=PER), :] for i in range(2)]
        swapped = [pltpu.roll(v, WIDE, 1) for v in pair]
        modes = [jnp.where(left, pair[0], swapped[1]), jnp.where(left, swapped[0], pair[1])]
        tiles.append(
            jnp.concatenate(
                [jnp.where((lane & 1) == reim, v, 0.0) for reim in range(2) for v in modes], 0
            )
        )
    gathered = jnp.concatenate(tiles, 1).astype(BF16)

    lhs = dot(perm_ref[...], gathered, NT)
    odd_row = odd_row_ref[...] > 0.5
    zero = jnp.zeros_like(lhs)
    lhs = jnp.concatenate(
        [jnp.where(odd_row, zero, lhs), jnp.where(odd_row, lhs, zero)], 1
    ).astype(BF16)

    width = 4096
    for p in range(PIX // width):
        at = slice(p * width, (p + 1) * width)
        table = tab_ref[:, at]
        maps = dot(lhs, table, NN)
        mix = [mix_ref[0, c, :, at] for c in range(COMPS)]
        diag = [diag_ref[0, e, :, at] for e in range(2)]
        cross = cross_ref[0, :, at]
        back = [[None] * PAIRS, [None] * PAIRS]
        for chain in range(CHAINS):
            sky = []
            for e in range(2):
                total = None
                for c in range(COMPS):
                    f = e * PAIRS + chain * COMPS + c
                    part = maps[f * PER : (f + 1) * PER] * mix[c]
                    total = part if total is None else total + part
                sky.append(total)
            weighted = [
                diag[0] * sky[0] + cross * sky[1],
                cross * sky[0] + diag[1] * sky[1],
            ]
            for e in range(2):
                for c in range(COMPS):
                    back[e][chain * COMPS + c] = weighted[e] * mix[c]
        back = jnp.concatenate(back[0] + back[1], 0).astype(BF16)
        part = dot(table, back, NT)
        if p == 0:
            acc_ref[...] = part
        else:
            acc_ref[...] += part

    odd_lane = jnp.concatenate([odd_lane_ref[...]] * 16, 0) > 0.5
    returned = jnp.where(odd_lane, acc_ref[128:, :], acc_ref[:128, :]).astype(BF16)
    spread = dot(returned, perm_ref[...], NN)
    for u in range(PER // 2):
        tile = spread[:, u * 128 : (u + 1) * 128]
        modes = [
            jnp.where((lane & 1) == 1, tile[64 + s * 32 : 96 + s * 32], tile[s * 32 : 32 + s * 32])
            for s in range(2)
        ]
        swapped = [pltpu.roll(v, WIDE, 1) for v in modes]
        rows_ref[pl.ds(2 * u, 32, stride=PER), :] = jnp.where(left, modes[0], swapped[1])
        rows_ref[pl.ds(2 * u + 1, 32, stride=PER), :] = jnp.where(left, swapped[0], modes[1])
    result = rows_ref[...].reshape(32, PER, 128)
    for c in range(2):
        out_ref[c] = (result + beam_ref[c][None]).reshape(256, 128).astype(BF16)
    for copy in copies:
        copy.wait()


def pixels(arrived, helpers, mixing, noise_diag, noise_cross, compact):
    vmem = pl.BlockSpec(memory_space=pltpu.VMEM)
    hbm = pl.BlockSpec(memory_space=pltpu.HBM)
    return pl.pallas_call(
        pixel_kernel,
        out_shape=(
            jax.ShapeDtypeStruct((2, 256, 128), BF16),
            jax.ShapeDtypeStruct(compact.shape, compact.dtype),
        ),
        in_specs=[vmem] * 9 + [hbm],
        out_specs=(vmem, vmem),
        scratch_shapes=[
            pltpu.VMEM((256, 128), F32),
            pltpu.VMEM((256, 2 * PAIRS * PER), F32),
            pltpu.SemaphoreType.DMA((CHUNKS,)),
        ],
        compiler_params=grant(10),
        name="pixels",
    )(arrived, *helpers, mixing, noise_diag, noise_cross, compact)


def gather_beam(stage_ref, beam_ref):
    parts = [stage_ref[pl.ds(i, 32, stride=PER), :] for i in range(3)]
    stage_ref[:32, :] = parts[0] + parts[1] + parts[2]
    lane = iota((8, 128), 1)
    total = jnp.zeros((8, 128), F32)
    for m in range(4):
        value = stage_ref[pl.ds(m, 8, stride=4), :]
        for i in range(2):
            source, place = COLS + i * WIDE, m * 32 + i * SPARE
            shift = (place - source) % 128
            moved = pltpu.roll(value, shift, 1) if shift else value
            total = jnp.where((lane >= place) & (lane < place + SPARE), moved, total)
    beam_ref[...] = total


def adjoint_kernel(
    core_ref, r_ref, tab_ref, out_ref, lhs_ref, plain_ref, cross_ref, stage_ref, beam_ref
):
    for b, index in enumerate((core_ref[0], 1 - core_ref[0])):
        stage_ref[b] = r_ref[index].astype(F32)
        for h in range(2):
            half = slice(h * 128, (h + 1) * 128)
            plain_ref[b, h] = stage_ref[b, half, :].T
            for k in range(4):
                value = plain_ref[b, h, pl.ds(3 - k, 32, stride=4), :]
                cross_ref[b, h, pl.ds(k, 32, stride=4), :] = SIGN[k] * value
            for s in range(2):
                at = slice(b * COLS, (b + 1) * COLS)
                rows = slice(s * WIDE, s * WIDE + COLS)
                lhs_ref[s, 0, at, half] = plain_ref[b, h, rows, :].astype(BF16)
                lhs_ref[s, 1, at, half] = cross_ref[b, h, rows, :].astype(BF16)
        gather_beam(stage_ref.at[b], beam_ref.at[b])

    width = 256
    for s in range(2):
        for k in range(tab_ref.shape[3] // width):
            at = slice(k * width, (k + 1) * width)
            sums = dot(lhs_ref[s, 0], tab_ref[s, 0, :, at], NN) + dot(
                lhs_ref[s, 1], tab_ref[s, 1, :, at], NN
            )
            for h in range(2):
                y = 2 * k + h
                part = sums[:, h * 128 : (h + 1) * 128]
                part = part[:COLS] * beam_ref[0, y : y + 1, :] + part[COLS:] * beam_ref[1, y : y + 1, :]
                out_ref[y, s] = part.astype(BF16)


def adjoint(core, returned, tables):
    cycles, levels = tables.shape[2:]
    blocks = levels // 128
    vmem = pl.BlockSpec(memory_space=pltpu.VMEM)
    return pl.pallas_call(
        adjoint_kernel,
        out_shape=jax.ShapeDtypeStruct((blocks, 2, COLS, 128), BF16),
        in_specs=[pl.BlockSpec(memory_space=pltpu.SMEM)] + [vmem] * 2,
        out_specs=vmem,
        scratch_shapes=[
            pltpu.VMEM((2, 2, 2 * COLS, cycles), BF16),
            pltpu.VMEM((2, 2, 128, 128), F32),
            pltpu.VMEM((2, 2, 128, 128), F32),
            pltpu.VMEM((2, cycles, 128), F32),
            pltpu.VMEM((2, blocks, 128), F32),
        ],
        compiler_params=grant(8),
        name="adjoint",
    )(core, returned, tables)


def final_kernel(band_ref, sum_ref, coef_ref, prior_ref, out_ref):
    kind = iota((COLS, 128), 0) % (4 * COMPS) // 2
    prior = jnp.zeros((COLS, 128), F32)
    for k in range(2 * COMPS):
        prior = jnp.where(kind == k, prior_ref[k : k + 1, :], prior)
    at = pl.ds(pl.multiple_of(128 * band_ref[0], 128), 128)
    for s in range(2):
        total = prior * coef_ref[s, :, at].astype(F32)
        for y in range(sum_ref.shape[0]):
            total = total + sum_ref[y, s].astype(F32)
        out_ref[s] = total


def final(band, gathered, coeffs_t, prior):
    vmem = pl.BlockSpec(memory_space=pltpu.VMEM)
    return pl.pallas_call(
        final_kernel,
        out_shape=jax.ShapeDtypeStruct((2, COLS, 128), F32),
        in_specs=[pl.BlockSpec(memory_space=pltpu.SMEM)] + [vmem] * 3,
        out_specs=vmem,
        compiler_params=grant(4),
        name="final",
    )(band, gathered, coeffs_t, prior)


def on_device(coeffs, tables, beam, mixing, noise_diag, noise_cross, prior, m_values, cycle_ids):
    core = lax.axis_index("core")
    band = (2 * lax.axis_index("y") + core).astype(jnp.int32)[None]
    core = core.astype(jnp.int32)[None]
    coeffs_t = coeffs.transpose(0, 2, 1)
    stored = pltpu.with_memory_space_constraint(tables, pltpu.HBM)
    spectra = synth(
        pltpu.with_memory_space_constraint(coeffs_t, pltpu.HBM),
        stored,
        pltpu.with_memory_space_constraint(beam, pltpu.HBM),
    )
    arrived = lax.all_to_all(spectra.reshape(32, PER, 128), "ma", 0, 0, tiled=True)
    part = lax.axis_index("ma").astype(jnp.int32)[None]
    *helpers, level_tables = phase_table(m_values, cycle_ids, core, band, part, beam, stored)
    arrived = arrived.reshape(256, 128)
    level_tables = pltpu.with_memory_space_constraint(level_tables, pltpu.HBM)
    returned, level_tables = pixels(
        arrived, helpers, mixing, noise_diag, noise_cross, level_tables
    )
    returned = lax.all_to_all(
        returned.reshape(64, PER, 128), ("core", "ma"), 0, 0, tiled=True
    ).reshape(2, 256, 128)
    partial = adjoint(core, returned, level_tables)
    gathered = lax.all_to_all(partial, "y", 0, 0, tiled=True)
    return final(band, gathered, coeffs_t, prior).transpose(0, 2, 1)


def solution(mesh):
    bands, modes = mesh.devices.shape
    fine = Mesh(mesh.devices.reshape(bands // 2, 2, modes), ("y", "core", "ma"))
    band = ("y", "core")
    in_specs = (
        P("ma", None, None),
        P("ma", None, None, None),
        P(band, None),
        P(band, None, "ma", None),
        P(band, None, "ma", None),
        P(band, "ma", None),
        P(None, band),
        P(),
        P("ma"),
    )
    return jax.shard_map(
        on_device, mesh=fine, in_specs=in_specs, out_specs=P("ma", band, None), check_vma=False
    )
```

```python
import math

import jax
import jax.numpy as jnp
from jax import lax
from jax.experimental import pallas as pl
from jax.experimental.pallas import tpu as pltpu
from jax.sharding import Mesh
from jax.sharding import PartitionSpec as P

F32 = jnp.float32
BF16 = jnp.bfloat16

PIX = 4096
COMPS = 3
CHAINS = 4
PAIRS = CHAINS * COMPS
COLS = 4 * PAIRS
WIDE = 64
SPARE = WIDE - COLS
PER = 8

NT = (((1,), (1,)), ((), ()))
NN = (((1,), (0,)), ((), ()))


def grant(mib):
    return pltpu.CompilerParams(vmem_limit_bytes=mib << 20)


def iota(shape, dim):
    return lax.broadcasted_iota(jnp.int32, shape, dim)


def dot(a, b, dims):
    return lax.dot_general(a, b, dims, preferred_element_type=F32)


SIGN = (-1.0, 1.0, 1.0, -1.0)


CHUNKS = 4


def synth_kernel(coef_hbm, tab_hbm, beam_hbm, out_ref, coef_ref, tab_ref, beam_ref, rows_ref, nat_ref, cross_ref, sems):
    levels = coef_ref.shape[2]
    width = levels // CHUNKS
    heads = [
        pltpu.make_async_copy(beam_hbm, beam_ref, sems.at[CHUNKS]),
        pltpu.make_async_copy(coef_hbm, coef_ref, sems.at[CHUNKS + 1]),
    ]
    for head in heads:
        head.start()
    copies = []
    for c in range(CHUNKS):
        at = pl.ds(c * width, width)
        copies.append(pltpu.make_async_copy(tab_hbm.at[:, :, :, at], tab_ref.at[c], sems.at[c]))
        copies[-1].start()
    rows_ref[...] = jnp.zeros_like(rows_ref)
    for head in heads:
        head.wait()
    for s in range(2):
        for j in range(levels // 128):
            at = slice(j * 128, (j + 1) * 128)
            beamed = (coef_ref[s, :, at].astype(F32) * beam_ref[:, at]).astype(BF16)
            rows_ref[s, 0, 0:COLS, at] = beamed
            nat_ref[s, j, :COLS, :] = beamed.astype(F32)
            for k in range(4):
                value = nat_ref[s, j, pl.ds(3 - k, PAIRS, stride=4), :]
                cross_ref[s, j, pl.ds(k, PAIRS, stride=4), :] = SIGN[k] * value
            rows_ref[s, 1, 0:COLS, at] = cross_ref[s, j].astype(BF16)
    total = [None, None]
    for c in range(CHUNKS):
        copies[c].wait()
        for s in range(2):
            for which in range(2):
                rows = rows_ref[s, which, :, c * width : (c + 1) * width]
                part = dot(tab_ref[c, s, which], rows, NT)
                total[s] = part if total[s] is None else total[s] + part
    out = jnp.concatenate(total, 1)
    out_ref[...] = out.astype(BF16)


def synth(coeffs_t, tables, beam):
    _, cols, levels = coeffs_t.shape
    cycles = tables.shape[2]
    hbm = pl.BlockSpec(memory_space=pltpu.HBM)
    vmem = pl.BlockSpec(memory_space=pltpu.VMEM)
    return pl.pallas_call(
        synth_kernel,
        out_shape=jax.ShapeDtypeStruct((cycles, 128), BF16),
        in_specs=[hbm] * 3,
        out_specs=vmem,
        scratch_shapes=[
            pltpu.VMEM((2, cols, levels), BF16),
            pltpu.VMEM((CHUNKS, 2, 2, cycles, levels // CHUNKS), BF16),
            pltpu.VMEM((1, levels), F32),
            pltpu.VMEM((2, 2, WIDE, levels), BF16),
            pltpu.VMEM((2, levels // 128, COLS, 128), F32),
            pltpu.VMEM((2, levels // 128, COLS, 128), F32),
            pltpu.SemaphoreType.DMA((CHUNKS + 2,)),
        ],
        compiler_params=grant(12),
        name="synth",
    )(coeffs_t, tables, beam)


def odd_cycle(ids_ref, place):
    odd = jnp.zeros(place.shape, F32)
    for t in range(PER):
        odd = jnp.where(place == t, (ids_ref[t] & 1).astype(F32), odd)
    return odd


def beam_rows(part, row):
    lane, sub = iota((8, 128), 1), iota((8, 128), 0)
    value = jnp.broadcast_to(row, (8, 128))
    start = (part % 4) * 32
    first = pltpu.roll(value, (128 + COLS - start) % 128, 1)
    second = pltpu.roll(value, (128 + COLS + WIDE - SPARE - start) % 128, 1)
    value = jnp.where(lane < WIDE, first, second)
    value = jnp.where((lane & (WIDE - 1)) >= COLS, value, 0.0)
    high = value.astype(BF16).astype(F32)
    middle = (value - high).astype(BF16).astype(F32)
    low = value - high - middle
    return jnp.where(sub == 0, high, jnp.where(sub == 1, middle, jnp.where(sub == 2, low, 0.0)))


def table_kernel(m_ref, ids_ref, core_ref, band_ref, part_ref, beam_ref, levels_hbm, *rest):
    out_ref, perm_ref, odd_row_ref, odd_lane_ref, rows_ref, compact_hbm, held_ref, sems = rest
    inward, outward = [], []
    for k in range(levels_hbm.shape[3] // 256):
        source = pl.ds(pl.multiple_of(256 * k + 128 * core_ref[0], 128), 128)
        place = pl.ds(128 * k, 128)
        held = held_ref.at[:, :, :, place]
        inward.append(
            pltpu.make_async_copy(levels_hbm.at[:, :, :, source], held, sems.at[0, k])
        )
        outward.append(
            pltpu.make_async_copy(held, compact_hbm.at[:, :, :, place], sems.at[1, k])
        )
        inward[-1].start()
    part = part_ref[0]
    for c in range(2):
        at = pl.ds(pl.multiple_of(256 * (part // 4) + 128 * c, 128), 128)
        rows_ref[c] = beam_rows(part, beam_ref[:, at])

    row, col = iota(perm_ref.shape, 0), iota(perm_ref.shape, 1)
    field = row // PER
    upper = (field >= PAIRS).astype(jnp.int32)
    target = (row % PER) * (WIDE // 2) + 2 * (field - PAIRS * upper) + upper
    perm_ref[...] = jnp.where((col >> 1) == target, 1.0, 0.0).astype(BF16)
    odd_row_ref[...] = odd_cycle(ids_ref, iota(odd_row_ref.shape, 0) % PER)
    odd_lane_ref[...] = odd_cycle(ids_ref, iota(odd_lane_ref.shape, 1) % PER)

    quarter = PIX // 4
    row = iota((32, 128), 0)
    mode, gain = [], []
    for s in range(2):
        m = jnp.zeros((32, 128), jnp.int32)
        for j in range(32):
            m = jnp.where(row == j, m_ref[2 * j + s], m)
        mode.append(m)
        gain.append(jnp.where(m == 0, 1.0, 2.0).astype(F32))
    lane = iota((32, 128), 1)

    def chunk(i, carry):
        first = i * 128
        for par in range(2):
            for s in range(2):
                k = (mode[s] * (2 * (lane + first) + par)) & (2 * PIX - 1)
                n = (k + quarter) >> 11
                angle = (k - (n << 11)).astype(F32) * F32(math.pi / PIX)
                sq = angle * angle
                c = -1 / 3628800
                for inv in (1 / 40320, -1 / 720, 1 / 24, -1 / 2, 1.0):
                    c = c * sq + F32(inv)
                d = 1 / 362880
                for inv in (-1 / 5040, 1 / 120, -1 / 6, 1.0):
                    d = d * sq + F32(inv)
                d = d * angle
                swap = (n & 1) == 1
                cosine = jnp.where(swap, d, c)
                sine = jnp.where(swap, c, d)
                cosine = jnp.where(((n + 1) & 2) == 2, -cosine, cosine)
                sine = jnp.where((n & 2) == 2, -sine, sine)
                for reim in range(2):
                    top = par * 128 + (2 * reim + s) * 32
                    for u in range(4):
                        turn = (mode[s] * u + reim) & 3
                        value = jnp.where((turn & 1) == 1, sine, cosine)
                        scale = jnp.where(((turn + 1) & 2) == 2, -gain[s], gain[s])
                        at = pl.ds(pl.multiple_of(u * quarter + first, 128), 128)
                        out_ref[top : top + 32, at] = (value * scale).astype(BF16)
        return carry

    lax.fori_loop(0, quarter // 256, chunk, 0)
    for k in range(len(inward)):
        inward[k].wait()
        outward[k].start()
    lax.fori_loop(quarter // 256, quarter // 128, chunk, 0)
    for copy in outward:
        copy.wait()


def phase_table(m_values, cycle_ids, core, band, part, beam, tables):
    rows = 2 * PAIRS * PER
    compact = tables.shape[:3] + (tables.shape[3] // 2,)
    smem = pl.BlockSpec(memory_space=pltpu.SMEM)
    vmem = pl.BlockSpec(memory_space=pltpu.VMEM)
    return pl.pallas_call(
        table_kernel,
        out_shape=(
            jax.ShapeDtypeStruct((256, PIX), BF16),
            jax.ShapeDtypeStruct((rows, WIDE * PER), BF16),
            jax.ShapeDtypeStruct((rows, 128), F32),
            jax.ShapeDtypeStruct((8, rows), F32),
            jax.ShapeDtypeStruct((2, 8, 128), F32),
            pltpu.HBM(compact, BF16),
        ),
        in_specs=[smem] * 5 + [vmem, pl.BlockSpec(memory_space=pltpu.HBM)],
        out_specs=[vmem] * 5 + [pl.BlockSpec(memory_space=pltpu.HBM)],
        scratch_shapes=[pltpu.VMEM(compact, BF16), pltpu.SemaphoreType.DMA((2, compact[3] // 128))],
        cost_estimate=pl.CostEstimate(flops=8_000_000, bytes_accessed=2_097_152, transcendentals=0),
        compiler_params=grant(8),
        name="phase_table",
    )(m_values, cycle_ids, core, band, part, beam, tables)


def pixel_kernel(x_ref, tab_ref, perm_ref, odd_row_ref, odd_lane_ref, beam_ref, *rest):
    mix_ref, diag_ref, cross_ref, compact_hbm, out_ref, levels_ref, rows_ref, acc_ref, sems = rest
    copies = []
    for k in range(2):
        at = pl.ds(k * compact_hbm.shape[3] // 2, compact_hbm.shape[3] // 2)
        source, place = compact_hbm.at[:, :, :, at], levels_ref.at[:, :, :, at]
        copies.append(pltpu.make_async_copy(source, place, sems.at[k]))
        copies[-1].start()
    lane = iota((32, 128), 1)
    left = lane < WIDE
    rows_ref[...] = x_ref[...].astype(F32)
    tiles = []
    for u in range(PER // 2):
        pair = [rows_ref[pl.ds(2 * u + i, 32, stride=PER), :] for i in range(2)]
        swapped = [pltpu.roll(v, WIDE, 1) for v in pair]
        modes = [jnp.where(left, pair[0], swapped[1]), jnp.where(left, swapped[0], pair[1])]
        tiles.append(
            jnp.concatenate(
                [jnp.where((lane & 1) == reim, v, 0.0) for reim in range(2) for v in modes], 0
            )
        )
    gathered = jnp.concatenate(tiles, 1).astype(BF16)

    lhs = dot(perm_ref[...], gathered, NT)
    odd_row = odd_row_ref[...] > 0.5
    zero = jnp.zeros_like(lhs)
    lhs = jnp.concatenate(
        [jnp.where(odd_row, zero, lhs), jnp.where(odd_row, lhs, zero)], 1
    ).astype(BF16)

    width = 4096
    for p in range(PIX // width):
        at = slice(p * width, (p + 1) * width)
        table = tab_ref[:, at]
        maps = dot(lhs, table, NN)
        mix = [mix_ref[0, c, :, at] for c in range(COMPS)]
        diag = [diag_ref[0, e, :, at] for e in range(2)]
        cross = cross_ref[0, :, at]
        back = [[None] * PAIRS, [None] * PAIRS]
        for chain in range(CHAINS):
            sky = []
            for e in range(2):
                total = None
                for c in range(COMPS):
                    f = e * PAIRS + chain * COMPS + c
                    part = maps[f * PER : (f + 1) * PER] * mix[c]
                    total = part if total is None else total + part
                sky.append(total)
            weighted = [
                diag[0] * sky[0] + cross * sky[1],
                cross * sky[0] + diag[1] * sky[1],
            ]
            for e in range(2):
                for c in range(COMPS):
                    back[e][chain * COMPS + c] = weighted[e] * mix[c]
        back = jnp.concatenate(back[0] + back[1], 0).astype(BF16)
        part = dot(table, back, NT)
        if p == 0:
            acc_ref[...] = part
        else:
            acc_ref[...] += part

    odd_lane = jnp.concatenate([odd_lane_ref[...]] * 16, 0) > 0.5
    returned = jnp.where(odd_lane, acc_ref[128:, :], acc_ref[:128, :]).astype(BF16)
    spread = dot(returned, perm_ref[...], NN)
    for u in range(PER // 2):
        tile = spread[:, u * 128 : (u + 1) * 128]
        modes = [
            jnp.where((lane & 1) == 1, tile[64 + s * 32 : 96 + s * 32], tile[s * 32 : 32 + s * 32])
            for s in range(2)
        ]
        swapped = [pltpu.roll(v, WIDE, 1) for v in modes]
        rows_ref[pl.ds(2 * u, 32, stride=PER), :] = jnp.where(left, modes[0], swapped[1])
        rows_ref[pl.ds(2 * u + 1, 32, stride=PER), :] = jnp.where(left, swapped[0], modes[1])
    result = rows_ref[...].reshape(32, PER, 128)
    for c in range(2):
        out_ref[c] = (result + beam_ref[c][None]).reshape(256, 128).astype(BF16)
    for copy in copies:
        copy.wait()


def pixels(arrived, helpers, mixing, noise_diag, noise_cross, compact):
    vmem = pl.BlockSpec(memory_space=pltpu.VMEM)
    hbm = pl.BlockSpec(memory_space=pltpu.HBM)
    return pl.pallas_call(
        pixel_kernel,
        out_shape=(
            jax.ShapeDtypeStruct((2, 256, 128), BF16),
            jax.ShapeDtypeStruct(compact.shape, compact.dtype),
        ),
        in_specs=[vmem] * 9 + [hbm],
        out_specs=(vmem, vmem),
        scratch_shapes=[
            pltpu.VMEM((256, 128), F32),
            pltpu.VMEM((256, 2 * PAIRS * PER), F32),
            pltpu.SemaphoreType.DMA((2,)),
        ],
        compiler_params=grant(10),
        name="pixels",
    )(arrived, *helpers, mixing, noise_diag, noise_cross, compact)


def gather_beam(stage_ref, beam_ref):
    parts = [stage_ref[pl.ds(i, 32, stride=PER), :] for i in range(3)]
    stage_ref[:32, :] = parts[0] + parts[1] + parts[2]
    lane = iota((8, 128), 1)
    total = jnp.zeros((8, 128), F32)
    for m in range(4):
        value = stage_ref[pl.ds(m, 8, stride=4), :]
        for i in range(2):
            source, place = COLS + i * WIDE, m * 32 + i * SPARE
            shift = (place - source) % 128
            moved = pltpu.roll(value, shift, 1) if shift else value
            total = jnp.where((lane >= place) & (lane < place + SPARE), moved, total)
    beam_ref[...] = total


def adjoint_kernel(
    core_ref, r_ref, tab_ref, out_ref, lhs_ref, plain_ref, cross_ref, stage_ref, beam_ref
):
    for b, index in enumerate((core_ref[0], 1 - core_ref[0])):
        stage_ref[b] = r_ref[index].astype(F32)
        for h in range(2):
            half = slice(h * 128, (h + 1) * 128)
            plain_ref[b, h] = stage_ref[b, half, :].T
            for k in range(4):
                value = plain_ref[b, h, pl.ds(3 - k, 32, stride=4), :]
                cross_ref[b, h, pl.ds(k, 32, stride=4), :] = SIGN[k] * value
            for s in range(2):
                at = slice(b * COLS, (b + 1) * COLS)
                rows = slice(s * WIDE, s * WIDE + COLS)
                lhs_ref[s, 0, at, half] = plain_ref[b, h, rows, :].astype(BF16)
                lhs_ref[s, 1, at, half] = cross_ref[b, h, rows, :].astype(BF16)
        gather_beam(stage_ref.at[b], beam_ref.at[b])

    width = 256
    for s in range(2):
        for k in range(tab_ref.shape[3] // width):
            at = slice(k * width, (k + 1) * width)
            sums = dot(lhs_ref[s, 0], tab_ref[s, 0, :, at], NN) + dot(
                lhs_ref[s, 1], tab_ref[s, 1, :, at], NN
            )
            for h in range(2):
                y = 2 * k + h
                part = sums[:, h * 128 : (h + 1) * 128]
                part = part[:COLS] * beam_ref[0, y : y + 1, :] + part[COLS:] * beam_ref[1, y : y + 1, :]
                out_ref[y, s] = part.astype(BF16)


def adjoint(core, returned, tables):
    cycles, levels = tables.shape[2:]
    blocks = levels // 128
    vmem = pl.BlockSpec(memory_space=pltpu.VMEM)
    return pl.pallas_call(
        adjoint_kernel,
        out_shape=jax.ShapeDtypeStruct((blocks, 2, COLS, 128), BF16),
        in_specs=[pl.BlockSpec(memory_space=pltpu.SMEM)] + [vmem] * 2,
        out_specs=vmem,
        scratch_shapes=[
            pltpu.VMEM((2, 2, 2 * COLS, cycles), BF16),
            pltpu.VMEM((2, 2, 128, 128), F32),
            pltpu.VMEM((2, 2, 128, 128), F32),
            pltpu.VMEM((2, cycles, 128), F32),
            pltpu.VMEM((2, blocks, 128), F32),
        ],
        compiler_params=grant(8),
        name="adjoint",
    )(core, returned, tables)


def final_kernel(band_ref, sum_ref, coef_ref, prior_ref, out_ref):
    kind = iota((COLS, 128), 0) % (4 * COMPS) // 2
    prior = jnp.zeros((COLS, 128), F32)
    for k in range(2 * COMPS):
        prior = jnp.where(kind == k, prior_ref[k : k + 1, :], prior)
    at = pl.ds(pl.multiple_of(128 * band_ref[0], 128), 128)
    for s in range(2):
        total = prior * coef_ref[s, :, at].astype(F32)
        for y in range(sum_ref.shape[0]):
            total = total + sum_ref[y, s].astype(F32)
        out_ref[s] = total


def final(band, gathered, coeffs_t, prior):
    vmem = pl.BlockSpec(memory_space=pltpu.VMEM)
    return pl.pallas_call(
        final_kernel,
        out_shape=jax.ShapeDtypeStruct((2, COLS, 128), F32),
        in_specs=[pl.BlockSpec(memory_space=pltpu.SMEM)] + [vmem] * 3,
        out_specs=vmem,
        compiler_params=grant(4),
        name="final",
    )(band, gathered, coeffs_t, prior)


def on_device(coeffs, tables, beam, mixing, noise_diag, noise_cross, prior, m_values, cycle_ids):
    core = lax.axis_index("core")
    band = (2 * lax.axis_index("y") + core).astype(jnp.int32)[None]
    core = core.astype(jnp.int32)[None]
    coeffs_t = coeffs.transpose(0, 2, 1)
    stored = pltpu.with_memory_space_constraint(tables, pltpu.HBM)
    spectra = synth(
        pltpu.with_memory_space_constraint(coeffs_t, pltpu.HBM),
        stored,
        pltpu.with_memory_space_constraint(beam, pltpu.HBM),
    )
    arrived = lax.all_to_all(spectra.reshape(32, PER, 128), "ma", 0, 0, tiled=True)
    part = lax.axis_index("ma").astype(jnp.int32)[None]
    *helpers, level_tables = phase_table(m_values, cycle_ids, core, band, part, beam, stored)
    arrived = arrived.reshape(256, 128)
    level_tables = pltpu.with_memory_space_constraint(level_tables, pltpu.HBM)
    returned, level_tables = pixels(
        arrived, helpers, mixing, noise_diag, noise_cross, level_tables
    )
    returned = lax.all_to_all(
        returned.reshape(64, PER, 128), ("core", "ma"), 0, 0, tiled=True
    ).reshape(2, 256, 128)
    partial = adjoint(core, returned, level_tables)
    gathered = lax.all_to_all(partial, "y", 0, 0, tiled=True)
    return final(band, gathered, coeffs_t, prior).transpose(0, 2, 1)


def solution(mesh):
    bands, modes = mesh.devices.shape
    fine = Mesh(mesh.devices.reshape(bands // 2, 2, modes), ("y", "core", "ma"))
    band = ("y", "core")
    in_specs = (
        P("ma", None, None),
        P("ma", None, None, None),
        P(band, None),
        P(band, None, "ma", None),
        P(band, None, "ma", None),
        P(band, "ma", None),
        P(None, band),
        P(),
        P("ma"),
    )
    return jax.shard_map(
        on_device, mesh=fine, in_specs=in_specs, out_specs=P("ma", band, None), check_vma=False
    )
```
